32 devices in a mesh: expert: 8 (over z, y), dp: 4 (over x, core).
Axes of the slice: x: 2, y: 2, z: 4, core: 2. Of those that a mesh axis runs over, the one named last changes fastest.
Arguments:
- tokens: bfloat16 [1024, 3584], P('expert', 'dp'), may hold values from -6 to 6
- expert_ids: int32 [1024, 8], P('expert'), may hold values from 0 to 15, all different within a row; in each aligned block of 128 rows (0 to 127, 128 to 255, ...) at most 128 rows name the same one
- gate_scales: float32 [1024, 8], P('expert'), may hold values from 0.05 to 0.5
- w_gate: bfloat16 [16, 3584, 1024], P('expert', 'dp'), may hold values from -0.09375 to 0.09375
- w_up: bfloat16 [16, 3584, 1024], P('expert', 'dp'), may hold values from -0.09375 to 0.09375
- w_down: bfloat16 [16, 1024, 3584], P('expert', None, 'dp'), may hold values from -0.1875 to 0.1875
Outputs:
- mixed: bfloat16 [1024, 3584], P('expert', 'dp')
The draws below stay inside these ranges and needn't reach their ends.
Inputs may be any that keep to these rules, and one draw needn't show every extreme that they name: `expert_ids`: each row names 8 different experts. In each aligned block of 128 rows (the rows of one index of expert) no expert is named by more than 128 rows, and in every draw some expert is named by exactly 128 rows of some block.
All inputs are finite; a program needn't handle non-finite values.
Results may differ from the reference program's by a relative error of at most 0.018.
Values may be sent and summed in bfloat16 or wider, within the bound.
A program may use at most 128 MiB of HBM per device.

```python
import math
import jax
import jax.numpy as jnp
import numpy as np
from jax import lax

D = 3584
FF = 1024
TOPK = 8
TOK_DEV = 128
EXPERTS = 16
TOKENS = 1024
CAP = 128
N_EXPERT = 8
N_DP = 4


def block_levels(key, dims, cuts, low, high):
    factor_of = 1.0
    for dim, parts in cuts:
        steps = jax.random.uniform(jax.random.fold_in(jax.random.fold_in(key, 6), dim), (parts,), jnp.float32, low / len(cuts), high / len(cuts))
        factor_of = factor_of * jnp.repeat(jnp.exp(steps), dims[dim] // parts).reshape((-1,) + (1,) * (len(dims) - 1 - dim))
    return factor_of


def deal_out(stream_key, own, number, rows, amount, top, limit, skew):
    sequence = jax.random.permutation(stream_key, amount)
    crowded, common = load_shares(amount, rows * top, limit, skew, True), load_shares(amount, rows * top, limit, skew, False)
    places = jnp.arange(amount)

    def named(sizes, offset_by):
        used = int((sizes > 0).sum())
        fixed = max(1, used // 4)
        passed = fixed + (places - fixed + offset_by * (used - fixed)) % max(1, amount - fixed)
        return jnp.zeros((amount,), jnp.int32).at[sequence[jnp.where(places < fixed, places, passed)]].set(jnp.asarray(sizes, jnp.int32))

    sizes = jnp.where(number % 4 == 0, named(crowded, number // 4), named(common, number - number // 4 - 1))
    mixed = jax.random.permutation(jax.random.fold_in(own, 3), amount)
    donor, receiver = mixed[0:amount // 2 * 2:2], mixed[1:amount // 2 * 2:2]
    room = jnp.minimum(sizes[donor] - 1, limit - sizes[receiver]) // 2
    room = jnp.where((donor == sequence[0]) | (receiver == sequence[0]) | (sizes[receiver] == 0), 0, jnp.maximum(room, 0))
    passed = jax.random.randint(jax.random.fold_in(own, 4), (amount // 2,), 0, 1 << 20) % (room + 1)
    sizes = sizes.at[donor].add(-passed).at[receiver].add(passed)
    labels = jnp.searchsorted(jnp.cumsum(sizes), jnp.arange(rows * top), side="right").astype(jnp.int32)
    table = labels.reshape(top, rows).T
    table = table[jax.random.permutation(jax.random.fold_in(own, 1), rows)]
    offset_by = jax.random.randint(jax.random.fold_in(own, 2), (rows, 1), 0, top)
    return jnp.take_along_axis(table, (jnp.arange(top)[None, :] + offset_by) % top, axis=1)


def load_shares(number_of, total, most, lean, full):
    portions = [(1 << 20) // math.isqrt(rank ** lean) + 1 for rank in range(1, number_of + 1)]
    largest = most if full else min(most, max(-(-total // number_of), total * portions[0] // sum(portions)))
    least = 1 if total - largest >= number_of - 1 else 0
    holding, spare = [largest] + [least] * (number_of - 1), total - largest - least * (number_of - 1)
    while spare > 0:
        movable = [i for i in range(1, number_of) if holding[i] < largest] or [i for i in range(1, number_of) if holding[i] < most]
        mass, remaining = sum([portions[i] for i in movable]), spare
        for i in movable:
            addition = min(most - holding[i], max(1, remaining * portions[i] // mass), spare)
            holding[i] = holding[i] + addition
            spare = spare - addition
    return np.array(holding)


def gaussian(stream_key, dims, scale, most, pieces=(), held_as=jnp.bfloat16):
    values = jax.random.normal(stream_key, dims, jnp.float32) * scale
    if len(pieces) > 0:
        values = block_levels(stream_key, dims, pieces, -0.22, 0.18) * values
    return jnp.clip(values, min=-most, max=most).astype(held_as)


def setup_inputs(seed: int = 0) -> dict:
    arg_keys = jax.random.split(jax.random.key(seed), 7)
    tokens = gaussian(arg_keys[0], (TOKENS, D), 1.0, 6.0, ((0, 8), (1, 4)))
    expert_ids_keys = jax.random.split(jax.random.fold_in(arg_keys[1], 1), TOKENS // TOK_DEV)
    expert_ids_turns = jax.random.permutation(jax.random.fold_in(arg_keys[1], 3), TOKENS // TOK_DEV)
    expert_ids = jax.vmap(lambda own, number: deal_out(jax.random.fold_in(arg_keys[1], 2), own, number, TOK_DEV, EXPERTS, TOPK, CAP, 2))(expert_ids_keys, expert_ids_turns).reshape((TOKENS, TOPK))
    gate_scales = jnp.clip(jnp.exp(math.log(0.5) - 2.3025851 * jax.random.uniform(arg_keys[2], (TOKENS, TOPK), jnp.float32) ** block_levels(arg_keys[2], (TOKENS, TOPK), ((0, 8),), -0.2, 0.2)), 0.05, 0.5)
    w_gate = gaussian(arg_keys[3], (EXPERTS, D, FF), D ** -0.5, 0.09375, ((0, 8), (1, 4)))
    w_up = gaussian(arg_keys[4], (EXPERTS, D, FF), D ** -0.5, 0.09375, ((0, 8), (1, 4)))
    w_down = gaussian(arg_keys[5], (EXPERTS, FF, D), FF ** -0.5, 0.1875, ((0, 8), (2, 4)))
    return {"tokens": tokens, "expert_ids": expert_ids, "gate_scales": gate_scales, "w_gate": w_gate, "w_up": w_up, "w_down": w_down}


def reference(tokens, expert_ids, gate_scales, w_gate, w_up, w_down):
    assigns = TOK_DEV * TOPK
    owner_rows = N_EXPERT * CAP
    slice_width = D // N_DP
    grouped = expert_ids.reshape(N_EXPERT, assigns)
    catalog = jnp.arange(EXPERTS, dtype=jnp.int32)
    onehot = (grouped[:, :, None] == catalog[None, None, :]).astype(jnp.int32)
    rank_in = jnp.sum((jnp.cumsum(onehot, axis=1) - 1) * onehot, axis=2).astype(jnp.int32)
    sources = jnp.arange(N_EXPERT, dtype=jnp.int32)[:, None]
    slot_index = (grouped * owner_rows + sources * CAP + rank_in).astype(jnp.int32)
    anchor = (sources * TOK_DEV + jnp.arange(assigns, dtype=jnp.int32)[None, :] // TOPK).astype(jnp.int32)
    lookup = jnp.full((EXPERTS * owner_rows,), TOKENS, jnp.int32).at[slot_index.reshape(-1)].set(anchor.reshape(-1))
    padded = jnp.concatenate([tokens, jnp.zeros((1, D), tokens.dtype)], axis=0)

    def run_expert(packed):
        rows_index, gate_here, up_here, down_here = packed
        rows_here = padded[rows_index].astype(jnp.float32).reshape(owner_rows, N_DP, slice_width)
        gate_parts = jnp.einsum("rnd,ndf->nrf", rows_here, gate_here.astype(jnp.float32).reshape(N_DP, slice_width, FF))
        up_parts = jnp.einsum("rnd,ndf->nrf", rows_here, up_here.astype(jnp.float32).reshape(N_DP, slice_width, FF))
        gate_sum = jnp.sum(lax.optimization_barrier(gate_parts.astype(jnp.bfloat16)).astype(jnp.float32), axis=0)
        up_sum = jnp.sum(lax.optimization_barrier(up_parts.astype(jnp.bfloat16)).astype(jnp.float32), axis=0)
        hidden = (jax.nn.silu(gate_sum) * up_sum).astype(jnp.bfloat16)
        return jnp.dot(hidden, down_here, preferred_element_type=jnp.float32).astype(jnp.bfloat16)

    expert_rows = lax.map(run_expert, (lookup.reshape(EXPERTS, owner_rows), w_gate, w_up, w_down))
    flat_rows = expert_rows.reshape(EXPERTS * owner_rows, D)
    chosen = slot_index.reshape(TOKENS, TOPK)
    mixed = jnp.zeros((TOKENS, D), jnp.float32)
    for which in range(TOPK):
        mixed = mixed + gate_scales[:, which:which + 1] * flat_rows[chosen[:, which]].astype(jnp.float32)
    return mixed.astype(jnp.bfloat16)
```

```python
import functools

import jax
import jax.numpy as jnp
from jax import lax
from jax.experimental import pallas as pl
from jax.experimental.pallas import tpu as pltpu
from jax.sharding import PartitionSpec as P


def running_count(hits):
    count = hits.shape[-2]
    upto = jnp.tril(jnp.ones((count, count), jnp.bfloat16))
    sums = jnp.einsum("ij,...jm->...im", upto, hits.astype(jnp.bfloat16), preferred_element_type=jnp.float32)
    return sums.astype(jnp.int32)


def routed_body(tokens, expert_ids, gate_scales, w_gate, w_up, w_down):
    tok_rows, slice_width = tokens.shape
    top_k = expert_ids.shape[1]
    source_count = lax.axis_size("expert")
    local_experts = w_gate.shape[0]
    hidden_units = w_gate.shape[2]
    experts_all = local_experts * source_count
    capacity = 2 * tok_rows * top_k // experts_all
    assigns = tok_rows * top_k
    owner_rows = source_count * capacity
    flat_ids = expert_ids.reshape(assigns)
    catalog = jnp.arange(experts_all, dtype=jnp.int32)
    onehot = (flat_ids[:, None] == catalog[None, :]).astype(jnp.int32)
    rank_in = jnp.sum((running_count(onehot) - 1) * onehot, axis=1)
    owners = flat_ids // local_experts
    within = flat_ids % local_experts
    slot_index = within * owner_rows + owners * capacity + rank_in
    every_token = lax.all_gather(tokens, "expert", axis=0, tiled=True)
    every_id = lax.all_gather(expert_ids, "expert", axis=0, tiled=True)
    my_index = lax.axis_index("expert")
    grouped = every_id.reshape(source_count, assigns) - my_index * local_experts
    my_hits = (
        grouped[:, :, None] == jnp.arange(local_experts, dtype=jnp.int32)[None, None, :]
    ).astype(jnp.int32)
    my_ranks = jnp.sum((running_count(my_hits) - 1) * my_hits, axis=2)
    hit_count = jnp.sum(my_hits, axis=2)
    sources = jnp.arange(source_count, dtype=jnp.int32)[:, None]
    target = jnp.where(
        hit_count > 0,
        grouped * owner_rows + sources * capacity + my_ranks,
        local_experts * owner_rows,
    )
    anchor = sources * tok_rows + jnp.arange(assigns, dtype=jnp.int32)[None, :] // top_k
    token_total = source_count * tok_rows
    lookup = (
        jnp.full((local_experts * owner_rows,), token_total, jnp.int32)
        .at[target.reshape(-1)]
        .set(anchor.reshape(-1), mode="drop")
    )
    padded = jnp.concatenate([every_token, jnp.zeros((1, slice_width), tokens.dtype)], axis=0)
    arrived = padded[lookup].reshape(local_experts, owner_rows, slice_width)
    outputs = []
    for local_index in range(local_experts):
        rows_here = arrived[local_index]
        gate_here = w_gate[local_index]
        up_here = w_up[local_index]
        down_here = w_down[local_index]
        gate_part = jnp.dot(rows_here, gate_here, preferred_element_type=jnp.float32)
        up_part = jnp.dot(rows_here, up_here, preferred_element_type=jnp.float32)
        summed = lax.psum_scatter(
            jnp.concatenate([gate_part, up_part], axis=1).astype(jnp.bfloat16),
            "dp",
            scatter_dimension=0,
            tiled=True,
        ).astype(jnp.float32)
        hidden = (jax.nn.silu(summed[:, :hidden_units]) * summed[:, hidden_units:]).astype(
            jnp.bfloat16
        )
        outputs.append(
            jnp.dot(
                lax.all_gather(hidden, "dp", axis=0, tiled=True),
                down_here,
                preferred_element_type=jnp.float32,
            ).astype(jnp.bfloat16)
        )
    results = jnp.stack(outputs).reshape(local_experts, source_count, capacity, slice_width)
    returned = lax.all_to_all(results, "expert", split_axis=1, concat_axis=1, tiled=True)
    returned = returned.reshape(local_experts * owner_rows, slice_width)
    picked = returned[slot_index].reshape(tok_rows, top_k, slice_width)
    mixed = jnp.sum(gate_scales[:, :, None] * picked.astype(jnp.float32), axis=1)
    return mixed.astype(jnp.bfloat16)


MESH = pl.DeviceIdType.MESH
(
    CORE, ACROSS, HIDDEN_ACROSS, HIDDEN_CORE, HIDDEN_FORWARD, TOKEN_LINE, TOKEN_PAIR,
    SCALE_LINE, SCALE_PAIR, RESULT_PAIR, RESULT_LINE,
) = range(11)

ORDER = (
    (0, 0, 0), (0, 1, 0),
    (1, 1, 0), (1, 1, 1),
    (2, 0, 0), (2, 0, 1), (2, 1, 0), (2, 1, 1),
    (3, 1, 0), (3, 1, 1), (3, 0, 0), (3, 0, 1),
    (1, 0, 0), (1, 0, 1),
    (0, 1, 1), (0, 0, 1),
)
RELAY = {1: ((1, 0),), 2: ((1, 1),), 4: ((2, 0),), 5: ((2, 1),), 6: ((3, 0),), 7: ((3, 1),)}
SEND = {2: ((2, 0), (2, 1)), 4: ((3, 0), (3, 1))}
LATE_PAIR = 8
MERGE_AT = 14
MERGE = ((2, 0), (2, 1), (3, 0), (3, 1), (1, 0), (1, 1))


def pick(index, table):
    value = jnp.int32(table[0])
    for place in range(1, len(table)):
        value = jnp.where(index >= place, jnp.int32(table[place]), value)
    return value


def peer_of(me, step):
    total = 0
    for bit in (1, 2, 4):
        total = total + bit * ((me // bit + step // bit) % 2)
    return total


def chunk_at(step):
    code = pick(step, [away * 4 + pair * 2 + part for away, pair, part in ORDER])
    return code // 4, code // 2 % 2, code % 2


def dense_kernel(
    tokens, ids, scales, w_gate, w_up, w_down, out,
    tok_buf, gate_v, up_v, down_v, scale_buf,
    core_send, core_recv, kept_part, across_send, across_recv, kept_sum,
    hidden, kept_result, pair_send, pair_recv, line_send, line_recv, weight_sem, send_sem, recv_sem,
):
    me = lax.axis_index("expert")
    slice_index = lax.axis_index("dp")
    core = slice_index % 2
    side = slice_index // 2
    other_core, other_side = 1 - core, 1 - side
    core_device = (me, side * 2 + other_core)
    side_device = (me, other_side * 2 + core)
    rows, width = tokens.shape
    part_rows = rows // 2
    half = hidden.shape[-1]
    line, steps = tok_buf.shape[0], core_send.shape[0]
    experts = scale_buf.shape[2]

    def load(place, source, target):
        return pltpu.make_async_copy(source, target, weight_sem.at[place])

    loads = [
        load(0, w_gate.at[other_core], gate_v.at[other_core]),
        load(1, w_up.at[other_core], up_v.at[other_core]),
        load(2, w_gate.at[core], gate_v.at[core]),
        load(3, w_up.at[core], up_v.at[core]),
        load(4, w_down, down_v),
    ]
    for each in loads:
        each.start()

    pair_device = (peer_of(me, 1), slice_index)

    def line_device(away):
        return (peer_of(me, 2 * away), slice_index)

    barrier = pltpu.get_barrier_semaphore()
    greeted = [core_device, side_device, pair_device] + [line_device(away) for away in range(1, line)]
    for device in greeted:
        pl.semaphore_signal(barrier, inc=1, device_id=device, device_id_type=MESH)

    for part in range(2):
        tok_buf[0, 0, part] = tokens[part * part_rows : (part + 1) * part_rows]
    which_expert = lax.broadcasted_iota(jnp.int32, (experts, rows), 0)
    table = jnp.zeros((experts, rows), jnp.float32)
    for k in range(ids.shape[0]):
        table = table + jnp.where(which_expert == ids[k : k + 1, :], scales[k : k + 1, :], 0.0)
    scale_buf[0, 0] = table

    pl.semaphore_wait(barrier, len(greeted))

    def copy(kind, step, source, target, device):
        return pltpu.make_async_remote_copy(
            src_ref=source,
            dst_ref=target,
            send_sem=send_sem.at[kind, step],
            recv_sem=recv_sem.at[kind, step],
            device_id=device,
            device_id_type=MESH,
        )

    def line_token(away, part):
        return copy(
            TOKEN_LINE, away * 2 + part, tok_buf.at[0, 0, part], tok_buf.at[away, 0, part], line_device(away)
        )

    def pair_token(away, part):
        return copy(
            TOKEN_PAIR, away * 2 + part, tok_buf.at[away, 0, part], tok_buf.at[away, 1, part], pair_device
        )

    def line_scale(away):
        return copy(SCALE_LINE, away, scale_buf.at[0, 0], scale_buf.at[away, 0], line_device(away))

    def pair_scale(away):
        return copy(SCALE_PAIR, away, scale_buf.at[away, 0], scale_buf.at[away, 1], pair_device)

    def core_copy(step):
        return copy(CORE, step, core_send.at[step], core_recv.at[step], core_device)

    def across_copy(step):
        return copy(ACROSS, step, across_send.at[step], across_recv.at[step], side_device)

    def hidden_copy(kind, step, owner, part, device):
        piece = hidden.at[step, owner, part]
        return copy(kind, step, piece, piece, device)

    def pair_result(away, part):
        return copy(
            RESULT_PAIR, away * 2 + part, pair_send.at[away, part], pair_recv.at[away, part], pair_device
        )

    def line_result(away, part):
        return copy(
            RESULT_LINE, away * 2 + part, line_send.at[away, part], line_recv.at[away, part], line_device(away)
        )

    pair_token(0, 0).start()
    line_token(1, 0).start()
    line_token(1, 1).start()
    pair_scale(0).start()
    for away in range(1, line):
        line_scale(away).start()

    def project_other(step, block):
        for which, weights in enumerate((gate_v, up_v)):
            for cut in range(2):
                core_send[step, which, cut] = jnp.dot(
                    block, weights[other_core, :, cut * half : (cut + 1) * half],
                    preferred_element_type=jnp.float32,
                ).astype(jnp.bfloat16)
        core_copy(step).start()

    def project_own(step, block):
        for which, weights in enumerate((gate_v, up_v)):
            for cut in range(2):
                kept_part[step % 2, which, cut] = jnp.dot(
                    block, weights[core, :, cut * half : (cut + 1) * half],
                    preferred_element_type=jnp.float32,
                )

    def project(step):
        away, pair, part = chunk_at(step)

        @pl.when(pair == 1)
        def _():
            pair_token(away, part).wait_recv()

        block = tok_buf[away, pair, part]
        project_other(step, block)
        project_own(step, block)

    def add_core(step):
        core_copy(step).wait_recv()
        slot = step % 2
        for which in range(2):
            across_send[step, which] = (
                kept_part[slot, which, other_side]
                + core_recv[step, which, other_side].astype(jnp.float32)
            ).astype(jnp.bfloat16)
        across_copy(step).start()
        for which in range(2):
            kept_sum[step % 3, which] = kept_part[slot, which, side] + core_recv[
                step, which, side
            ].astype(jnp.float32)

    def activate(step):
        away, pair, part = chunk_at(step)

        @pl.when((part == 0) & (pair == 1))
        def _():
            pair_scale(away).wait_recv()

        across_copy(step).wait_recv()
        slot = step % 3
        shape = (part_rows, rows)
        chosen = lax.broadcasted_iota(jnp.int32, shape, 0) + part * part_rows == (
            lax.broadcasted_iota(jnp.int32, shape, 1)
        )
        row = scale_buf[away, pair, pl.ds(2 * me + core, 1), :]
        scale = jnp.sum(jnp.where(chosen, row, 0.0), axis=1, keepdims=True)
        gate = kept_sum[slot, 0] + across_recv[step, 0].astype(jnp.float32)
        up = kept_sum[slot, 1] + across_recv[step, 1].astype(jnp.float32)
        hidden[step, core, side] = (gate / (1.0 + jnp.exp(-gate)) * up * scale).astype(jnp.bfloat16)
        hidden_copy(HIDDEN_ACROSS, step, core, side, side_device).start()
        hidden_copy(HIDDEN_CORE, step, core, side, core_device).start()

    def forward(step):
        hidden_copy(HIDDEN_ACROSS, step, core, other_side, side_device).wait_recv()
        hidden_copy(HIDDEN_FORWARD, step, core, other_side, core_device).start()

    def finish(step):
        away, pair, part = chunk_at(step)

        @pl.when(step == 0)
        def _():
            loads[4].wait()

        hidden_copy(HIDDEN_CORE, step, other_core, side, core_device).wait_recv()
        hidden_copy(HIDDEN_FORWARD, step, other_core, other_side, core_device).wait_recv()
        pieces = [hidden[step, owner, cut] for owner in range(2) for cut in range(2)]
        middle = width // 256 * 128
        for low, high in ((0, middle), (middle, width)):
            value = sum(
                jnp.dot(
                    pieces[2 * owner + cut],
                    down_v[owner, cut * half : (cut + 1) * half, low:high],
                    preferred_element_type=jnp.float32,
                )
                for owner in range(2)
                for cut in range(2)
            )

            @pl.when(pair == 0)
            def _():
                kept_result[away, part, :, low:high] = value

            @pl.when(pair == 1)
            def _():
                pair_send[away, part, :, low:high] = value.astype(jnp.bfloat16)

        @pl.when(pair == 1)
        def _():
            pair_result(away, part).start()

    def merge(place):
        away, part = pick(place, [entry[0] for entry in MERGE]), place % 2
        pair_result(away, part).wait_recv()
        line_send[away, part] = (
            kept_result[away, part] + pair_recv[away, part].astype(jnp.float32)
        ).astype(jnp.bfloat16)
        line_result(away, part).start()

    def conclude(part):
        pair_result(0, part).wait_recv()
        value = kept_result[0, part] + pair_recv[0, part].astype(jnp.float32)
        for away in (2, 3, 1):
            line_result(away, part).wait_recv()
            value = value + line_recv[away, part].astype(jnp.float32)
        out[part * part_rows : (part + 1) * part_rows] = value.astype(out.dtype)

    loads[0].wait()
    loads[1].wait()
    project_other(0, tok_buf[0, 0, 0])
    loads[2].wait()
    loads[3].wait()
    project_own(0, tok_buf[0, 0, 0])

    def staged(turn, lag, stage):
        @pl.when((turn >= lag) & (turn < steps + lag))
        def _():
            stage(turn - lag)

    def iteration(turn, carry):
        staged(turn, 1, add_core)
        for at, entries in RELAY.items():
            @pl.when(turn == at)
            def _():
                for away, part in entries:
                    line_token(away, part).wait_recv()
                    pair_token(away, part).start()
                    if part == 0:
                        line_scale(away).wait_recv()
                        pair_scale(away).start()
        for at, entries in SEND.items():
            @pl.when(turn == at)
            def _():
                for away, part in entries:
                    line_token(away, part).start()

        @pl.when(turn == LATE_PAIR)
        def _():
            pair_token(0, 1).start()

        staged(turn, 0, project)
        staged(turn, 3, activate)
        staged(turn, 5, forward)
        staged(turn, 6, finish)

        @pl.when((turn >= MERGE_AT) & (turn < MERGE_AT + len(MERGE)))
        def _():
            merge(turn - MERGE_AT)

        return carry

    lax.fori_loop(1, steps + 6, iteration, 0)

    for part in range(2):
        conclude(part)

    def drain(step, carry):
        core_copy(step).wait_send()
        across_copy(step).wait_send()
        hidden_copy(HIDDEN_ACROSS, step, core, side, side_device).wait_send()
        hidden_copy(HIDDEN_CORE, step, core, side, core_device).wait_send()
        hidden_copy(HIDDEN_FORWARD, step, core, other_side, core_device).wait_send()
        return carry

    lax.fori_loop(0, steps, drain, 0)
    for away in range(line):
        pair_scale(away).wait_send()
        if away > 0:
            line_scale(away).wait_send()
        for part in range(2):
            pair_token(away, part).wait_send()
            pair_result(away, part).wait_send()
            if away > 0:
                line_token(away, part).wait_send()
                line_result(away, part).wait_send()


def dense_body(tokens, expert_ids, gate_scales, w_gate, w_up, w_down):
    rows, width = tokens.shape
    sources = lax.axis_size("expert")
    line, steps, part_rows = sources // 2, 2 * sources, rows // 2
    experts = w_gate.shape[0] * sources
    half = w_gate.shape[2] // 2
    narrow, wide = jnp.bfloat16, jnp.float32
    vmem, anywhere = pl.BlockSpec(memory_space=pltpu.VMEM), pl.BlockSpec(memory_space=pl.ANY)
    return pl.pallas_call(
        dense_kernel,
        out_shape=jax.ShapeDtypeStruct((rows, width), narrow),
        in_specs=[vmem, vmem, vmem, anywhere, anywhere, anywhere],
        out_specs=vmem,
        scratch_shapes=[
            pltpu.VMEM((line, 2, 2, part_rows, width), narrow),
            pltpu.VMEM(w_gate.shape, narrow),
            pltpu.VMEM(w_up.shape, narrow),
            pltpu.VMEM(w_down.shape, narrow),
            pltpu.VMEM((line, 2, experts, rows), wide),
            pltpu.VMEM((steps, 2, 2, part_rows, half), narrow),
            pltpu.VMEM((steps, 2, 2, part_rows, half), narrow),
            pltpu.VMEM((2, 2, 2, part_rows, half), wide),
            pltpu.VMEM((steps, 2, part_rows, half), narrow),
            pltpu.VMEM((steps, 2, part_rows, half), narrow),
            pltpu.VMEM((3, 2, part_rows, half), wide),
            pltpu.VMEM((steps, 2, 2, part_rows, half), narrow),
            pltpu.VMEM((line, 2, part_rows, width), wide),
            pltpu.VMEM((line, 2, part_rows, width), narrow),
            pltpu.VMEM((line, 2, part_rows, width), narrow),
            pltpu.VMEM((line, 2, part_rows, width), narrow),
            pltpu.VMEM((line, 2, part_rows, width), narrow),
            pltpu.SemaphoreType.DMA((5,)),
            pltpu.SemaphoreType.DMA((11, steps)),
            pltpu.SemaphoreType.DMA((11, steps)),
        ],
        compiler_params=pltpu.CompilerParams(
            collective_id=0, has_side_effects=True, vmem_limit_bytes=56 * 2**20
        ),
    )(tokens, expert_ids.T, gate_scales.T, w_gate, w_up, w_down)


def body(tokens, expert_ids, gate_scales, w_gate, w_up, w_down):
    rows, top_k = expert_ids.shape
    sources = lax.axis_size("expert")
    experts_all = w_gate.shape[0] * sources
    every_slot_used = 2 * rows * top_k // experts_all >= rows
    grouped = w_gate.shape[0] == 2 and lax.axis_size("dp") == 4 and sources == 8
    chosen = dense_body if every_slot_used and grouped else routed_body
    return chosen(tokens, expert_ids, gate_scales, w_gate, w_up, w_down)


def solution(mesh):
    in_specs = (
        P("expert", "dp"),
        P("expert", None),
        P("expert", None),
        P("expert", "dp", None),
        P("expert", "dp", None),
        P("expert", None, "dp"),
    )
    out_specs = P("expert", "dp")
    return jax.shard_map(body, mesh=mesh, in_specs=in_specs, out_specs=out_specs, check_vma=False)
```

```python
import functools

import jax
import jax.numpy as jnp
from jax import lax
from jax.experimental import pallas as pl
from jax.experimental.pallas import tpu as pltpu
from jax.sharding import PartitionSpec as P


def running_count(hits):
    count = hits.shape[-2]
    upto = jnp.tril(jnp.ones((count, count), jnp.bfloat16))
    sums = jnp.einsum("ij,...jm->...im", upto, hits.astype(jnp.bfloat16), preferred_element_type=jnp.float32)
    return sums.astype(jnp.int32)


def routed_body(tokens, expert_ids, gate_scales, w_gate, w_up, w_down):
    tok_rows, slice_width = tokens.shape
    top_k = expert_ids.shape[1]
    source_count = lax.axis_size("expert")
    local_experts = w_gate.shape[0]
    hidden_units = w_gate.shape[2]
    experts_all = local_experts * source_count
    capacity = 2 * tok_rows * top_k // experts_all
    assigns = tok_rows * top_k
    owner_rows = source_count * capacity
    flat_ids = expert_ids.reshape(assigns)
    catalog = jnp.arange(experts_all, dtype=jnp.int32)
    onehot = (flat_ids[:, None] == catalog[None, :]).astype(jnp.int32)
    rank_in = jnp.sum((running_count(onehot) - 1) * onehot, axis=1)
    owners = flat_ids // local_experts
    within = flat_ids % local_experts
    slot_index = within * owner_rows + owners * capacity + rank_in
    every_token = lax.all_gather(tokens, "expert", axis=0, tiled=True)
    every_id = lax.all_gather(expert_ids, "expert", axis=0, tiled=True)
    my_index = lax.axis_index("expert")
    grouped = every_id.reshape(source_count, assigns) - my_index * local_experts
    my_hits = (
        grouped[:, :, None] == jnp.arange(local_experts, dtype=jnp.int32)[None, None, :]
    ).astype(jnp.int32)
    my_ranks = jnp.sum((running_count(my_hits) - 1) * my_hits, axis=2)
    hit_count = jnp.sum(my_hits, axis=2)
    sources = jnp.arange(source_count, dtype=jnp.int32)[:, None]
    target = jnp.where(
        hit_count > 0,
        grouped * owner_rows + sources * capacity + my_ranks,
        local_experts * owner_rows,
    )
    anchor = sources * tok_rows + jnp.arange(assigns, dtype=jnp.int32)[None, :] // top_k
    token_total = source_count * tok_rows
    lookup = (
        jnp.full((local_experts * owner_rows,), token_total, jnp.int32)
        .at[target.reshape(-1)]
        .set(anchor.reshape(-1), mode="drop")
    )
    padded = jnp.concatenate([every_token, jnp.zeros((1, slice_width), tokens.dtype)], axis=0)
    arrived = padded[lookup].reshape(local_experts, owner_rows, slice_width)
    outputs = []
    for local_index in range(local_experts):
        rows_here = arrived[local_index]
        gate_here = w_gate[local_index]
        up_here = w_up[local_index]
        down_here = w_down[local_index]
        gate_part = jnp.dot(rows_here, gate_here, preferred_element_type=jnp.float32)
        up_part = jnp.dot(rows_here, up_here, preferred_element_type=jnp.float32)
        summed = lax.psum_scatter(
            jnp.concatenate([gate_part, up_part], axis=1).astype(jnp.bfloat16),
            "dp",
            scatter_dimension=0,
            tiled=True,
        ).astype(jnp.float32)
        hidden = (jax.nn.silu(summed[:, :hidden_units]) * summed[:, hidden_units:]).astype(
            jnp.bfloat16
        )
        outputs.append(
            jnp.dot(
                lax.all_gather(hidden, "dp", axis=0, tiled=True),
                down_here,
                preferred_element_type=jnp.float32,
            ).astype(jnp.bfloat16)
        )
    results = jnp.stack(outputs).reshape(local_experts, source_count, capacity, slice_width)
    returned = lax.all_to_all(results, "expert", split_axis=1, concat_axis=1, tiled=True)
    returned = returned.reshape(local_experts * owner_rows, slice_width)
    picked = returned[slot_index].reshape(tok_rows, top_k, slice_width)
    mixed = jnp.sum(gate_scales[:, :, None] * picked.astype(jnp.float32), axis=1)
    return mixed.astype(jnp.bfloat16)


MESH = pl.DeviceIdType.MESH
(
    CORE, ACROSS, HIDDEN_ACROSS, HIDDEN_CORE, HIDDEN_FORWARD, TOKEN_LINE, TOKEN_PAIR,
    SCALE_LINE, SCALE_PAIR, RESULT_PAIR, RESULT_LINE,
) = range(11)

ORDER = (
    (0, 0, 0), (0, 0, 1), (0, 1, 0),
    (1, 1, 0), (1, 1, 1),
    (2, 0, 0), (2, 0, 1), (2, 1, 0), (2, 1, 1),
    (3, 1, 0), (3, 1, 1), (3, 0, 0), (3, 0, 1),
    (1, 0, 0), (1, 0, 1),
    (0, 1, 1),
)
RELAY = {2: ((1, 0),), 3: ((1, 1),), 5: ((2, 0),), 6: ((2, 1),), 8: ((3, 0),), 9: ((3, 1),)}
SEND = {1: ((1, 1),), 3: ((2, 0),), 4: ((2, 1),), 6: ((3, 0),), 7: ((3, 1),)}
LATE_PAIR = 8
MERGE_AT = 15
MERGE = ((2, 0), (2, 1), (3, 0), (3, 1), (1, 0), (1, 1))


def pick(index, table):
    value = jnp.int32(table[0])
    for place in range(1, len(table)):
        value = jnp.where(index >= place, jnp.int32(table[place]), value)
    return value


def peer_of(me, step):
    total = 0
    for bit in (1, 2, 4):
        total = total + bit * ((me // bit + step // bit) % 2)
    return total


def chunk_at(step):
    code = pick(step, [away * 4 + pair * 2 + part for away, pair, part in ORDER])
    return code // 4, code // 2 % 2, code % 2


def dense_kernel(
    tokens, ids, scales, w_gate, w_up, w_down, out,
    tok_buf, gate_v, up_v, down_v, scale_buf,
    core_send, core_recv, kept_part, across_send, across_recv, kept_sum,
    hidden, kept_result, pair_send, pair_recv, line_send, line_recv, weight_sem, send_sem, recv_sem,
):
    me = lax.axis_index("expert")
    slice_index = lax.axis_index("dp")
    core = slice_index % 2
    side = slice_index // 2
    other_core, other_side = 1 - core, 1 - side
    core_device = (me, side * 2 + other_core)
    side_device = (me, other_side * 2 + core)
    rows, width = tokens.shape
    part_rows = rows // 2
    half = hidden.shape[-1]
    line, steps = tok_buf.shape[0], core_send.shape[0]
    experts = scale_buf.shape[2]

    def load(place, source, target):
        return pltpu.make_async_copy(source, target, weight_sem.at[place])

    loads = [
        load(0, w_gate.at[other_core], gate_v.at[other_core]),
        load(1, w_up.at[other_core], up_v.at[other_core]),
        load(2, w_gate.at[core], gate_v.at[core]),
        load(3, w_up.at[core], up_v.at[core]),
        load(4, w_down, down_v),
    ]
    for each in loads:
        each.start()

    pair_device = (peer_of(me, 1), slice_index)

    def line_device(away):
        return (peer_of(me, 2 * away), slice_index)

    barrier = pltpu.get_barrier_semaphore()
    greeted = [core_device, side_device, pair_device] + [line_device(away) for away in range(1, line)]
    for device in greeted:
        pl.semaphore_signal(barrier, inc=1, device_id=device, device_id_type=MESH)

    for part in range(2):
        tok_buf[0, 0, part] = tokens[part * part_rows : (part + 1) * part_rows]
    which_expert = lax.broadcasted_iota(jnp.int32, (experts, rows), 0)
    table = jnp.zeros((experts, rows), jnp.float32)
    for k in range(ids.shape[0]):
        table = table + jnp.where(which_expert == ids[k : k + 1, :], scales[k : k + 1, :], 0.0)
    scale_buf[0, 0] = table

    pl.semaphore_wait(barrier, len(greeted))

    def copy(kind, step, source, target, device):
        return pltpu.make_async_remote_copy(
            src_ref=source,
            dst_ref=target,
            send_sem=send_sem.at[kind, step],
            recv_sem=recv_sem.at[kind, step],
            device_id=device,
            device_id_type=MESH,
        )

    def line_token(away, part):
        return copy(
            TOKEN_LINE, away * 2 + part, tok_buf.at[0, 0, part], tok_buf.at[away, 0, part], line_device(away)
        )

    def pair_token(away, part):
        return copy(
            TOKEN_PAIR, away * 2 + part, tok_buf.at[away, 0, part], tok_buf.at[away, 1, part], pair_device
        )

    def line_scale(away):
        return copy(SCALE_LINE, away, scale_buf.at[0, 0], scale_buf.at[away, 0], line_device(away))

    def pair_scale(away):
        return copy(SCALE_PAIR, away, scale_buf.at[away, 0], scale_buf.at[away, 1], pair_device)

    def core_copy(step):
        return copy(CORE, step, core_send.at[step], core_recv.at[step], core_device)

    def across_copy(step):
        return copy(ACROSS, step, across_send.at[step], across_recv.at[step], side_device)

    def hidden_copy(kind, step, owner, part, device):
        piece = hidden.at[step, owner, part]
        return copy(kind, step, piece, piece, device)

    def pair_result(away, part):
        return copy(
            RESULT_PAIR, away * 2 + part, pair_send.at[away, part], pair_recv.at[away, part], pair_device
        )

    def line_result(away, part):
        return copy(
            RESULT_LINE, away * 2 + part, line_send.at[away, part], line_recv.at[away, part], line_device(away)
        )

    pair_token(0, 0).start()
    line_token(1, 0).start()
    pair_scale(0).start()
    for away in range(1, line):
        line_scale(away).start()

    def project_other(step, block):
        for which, weights in enumerate((gate_v, up_v)):
            for cut in range(2):
                core_send[step, which, cut] = jnp.dot(
                    block, weights[other_core, :, cut * half : (cut + 1) * half],
                    preferred_element_type=jnp.float32,
                ).astype(jnp.bfloat16)
        core_copy(step).start()

    def project_own(step, block):
        for which, weights in enumerate((gate_v, up_v)):
            for cut in range(2):
                kept_part[step % 2, which, cut] = jnp.dot(
                    block, weights[core, :, cut * half : (cut + 1) * half],
                    preferred_element_type=jnp.float32,
                )

    def project(step):
        away, pair, part = chunk_at(step)

        @pl.when(pair == 1)
        def _():
            pair_token(away, part).wait_recv()

        block = tok_buf[away, pair, part]
        project_other(step, block)
        project_own(step, block)

    def add_core(step):
        core_copy(step).wait_recv()
        slot = step % 2
        for which in range(2):
            across_send[step, which] = (
                kept_part[slot, which, other_side]
                + core_recv[step, which, other_side].astype(jnp.float32)
            ).astype(jnp.bfloat16)
        across_copy(step).start()
        for which in range(2):
            kept_sum[step % 3, which] = kept_part[slot, which, side] + core_recv[
                step, which, side
            ].astype(jnp.float32)

    def activate(step):
        away, pair, part = chunk_at(step)

        @pl.when((part == 0) & (pair == 1))
        def _():
            pair_scale(away).wait_recv()

        across_copy(step).wait_recv()
        slot = step % 3
        shape = (part_rows, rows)
        chosen = lax.broadcasted_iota(jnp.int32, shape, 0) + part * part_rows == (
            lax.broadcasted_iota(jnp.int32, shape, 1)
        )
        row = scale_buf[away, pair, pl.ds(2 * me + core, 1), :]
        scale = jnp.sum(jnp.where(chosen, row, 0.0), axis=1, keepdims=True)
        gate = kept_sum[slot, 0] + across_recv[step, 0].astype(jnp.float32)
        up = kept_sum[slot, 1] + across_recv[step, 1].astype(jnp.float32)
        hidden[step, core, side] = (gate / (1.0 + jnp.exp(-gate)) * up * scale).astype(jnp.bfloat16)
        hidden_copy(HIDDEN_ACROSS, step, core, side, side_device).start()
        hidden_copy(HIDDEN_CORE, step, core, side, core_device).start()

    def forward(step):
        hidden_copy(HIDDEN_ACROSS, step, core, other_side, side_device).wait_recv()
        hidden_copy(HIDDEN_FORWARD, step, core, other_side, core_device).start()

    def finish(step):
        away, pair, part = chunk_at(step)

        @pl.when(step == 0)
        def _():
            loads[4].wait()

        hidden_copy(HIDDEN_CORE, step, other_core, side, core_device).wait_recv()
        hidden_copy(HIDDEN_FORWARD, step, other_core, other_side, core_device).wait_recv()
        pieces = [hidden[step, owner, cut] for owner in range(2) for cut in range(2)]
        middle = width // 256 * 128
        for low, high in ((0, middle), (middle, width)):
            value = sum(
                jnp.dot(
                    pieces[2 * owner + cut],
                    down_v[owner, cut * half : (cut + 1) * half, low:high],
                    preferred_element_type=jnp.float32,
                )
                for owner in range(2)
                for cut in range(2)
            )

            @pl.when(pair == 0)
            def _():
                kept_result[away, part, :, low:high] = value

            @pl.when(pair == 1)
            def _():
                pair_send[away, part, :, low:high] = value.astype(jnp.bfloat16)

        @pl.when(pair == 1)
        def _():
            pair_result(away, part).start()

    def merge(place):
        away, part = pick(place, [entry[0] for entry in MERGE]), place % 2
        pair_result(away, part).wait_recv()
        line_send[away, part] = (
            kept_result[away, part] + pair_recv[away, part].astype(jnp.float32)
        ).astype(jnp.bfloat16)
        line_result(away, part).start()

    def conclude(part):
        pair_result(0, part).wait_recv()
        value = kept_result[0, part] + pair_recv[0, part].astype(jnp.float32)
        for away in (2, 3, 1):
            line_result(away, part).wait_recv()
            value = value + line_recv[away, part].astype(jnp.float32)
        out[part * part_rows : (part + 1) * part_rows] = value.astype(out.dtype)

    loads[0].wait()
    loads[1].wait()
    project_other(0, tok_buf[0, 0, 0])
    loads[2].wait()
    loads[3].wait()
    project_own(0, tok_buf[0, 0, 0])

    def staged(turn, lag, stage):
        @pl.when((turn >= lag) & (turn < steps + lag))
        def _():
            stage(turn - lag)

    def iteration(turn, carry):
        staged(turn, 1, add_core)
        for at, entries in RELAY.items():
            @pl.when(turn == at)
            def _():
                for away, part in entries:
                    line_token(away, part).wait_recv()
                    pair_token(away, part).start()
                    if part == 0:
                        line_scale(away).wait_recv()
                        pair_scale(away).start()
        for at, entries in SEND.items():
            @pl.when(turn == at)
            def _():
                for away, part in entries:
                    line_token(away, part).start()

        @pl.when(turn == LATE_PAIR)
        def _():
            pair_token(0, 1).start()

        staged(turn, 0, project)
        staged(turn, 3, activate)
        staged(turn, 5, forward)
        staged(turn, 6, finish)

        @pl.when((turn >= MERGE_AT) & (turn < MERGE_AT + len(MERGE)))
        def _():
            merge(turn - MERGE_AT)

        return carry

    lax.fori_loop(1, steps + 6, iteration, 0)

    for part in range(2):
        conclude(part)

    def drain(step, carry):
        core_copy(step).wait_send()
        across_copy(step).wait_send()
        hidden_copy(HIDDEN_ACROSS, step, core, side, side_device).wait_send()
        hidden_copy(HIDDEN_CORE, step, core, side, core_device).wait_send()
        hidden_copy(HIDDEN_FORWARD, step, core, other_side, core_device).wait_send()
        return carry

    lax.fori_loop(0, steps, drain, 0)
    for away in range(line):
        pair_scale(away).wait_send()
        if away > 0:
            line_scale(away).wait_send()
        for part in range(2):
            pair_token(away, part).wait_send()
            pair_result(away, part).wait_send()
            if away > 0:
                line_token(away, part).wait_send()
                line_result(away, part).wait_send()


def dense_body(tokens, expert_ids, gate_scales, w_gate, w_up, w_down):
    rows, width = tokens.shape
    sources = lax.axis_size("expert")
    line, steps, part_rows = sources // 2, 2 * sources, rows // 2
    experts = w_gate.shape[0] * sources
    half = w_gate.shape[2] // 2
    narrow, wide = jnp.bfloat16, jnp.float32
    vmem, anywhere = pl.BlockSpec(memory_space=pltpu.VMEM), pl.BlockSpec(memory_space=pl.ANY)
    return pl.pallas_call(
        dense_kernel,
        out_shape=jax.ShapeDtypeStruct((rows, width), narrow),
        in_specs=[vmem, vmem, vmem, anywhere, anywhere, anywhere],
        out_specs=vmem,
        scratch_shapes=[
            pltpu.VMEM((line, 2, 2, part_rows, width), narrow),
            pltpu.VMEM(w_gate.shape, narrow),
            pltpu.VMEM(w_up.shape, narrow),
            pltpu.VMEM(w_down.shape, narrow),
            pltpu.VMEM((line, 2, experts, rows), wide),
            pltpu.VMEM((steps, 2, 2, part_rows, half), narrow),
            pltpu.VMEM((steps, 2, 2, part_rows, half), narrow),
            pltpu.VMEM((2, 2, 2, part_rows, half), wide),
            pltpu.VMEM((steps, 2, part_rows, half), narrow),
            pltpu.VMEM((steps, 2, part_rows, half), narrow),
            pltpu.VMEM((3, 2, part_rows, half), wide),
            pltpu.VMEM((steps, 2, 2, part_rows, half), narrow),
            pltpu.VMEM((line, 2, part_rows, width), wide),
            pltpu.VMEM((line, 2, part_rows, width), narrow),
            pltpu.VMEM((line, 2, part_rows, width), narrow),
            pltpu.VMEM((line, 2, part_rows, width), narrow),
            pltpu.VMEM((line, 2, part_rows, width), narrow),
            pltpu.SemaphoreType.DMA((5,)),
            pltpu.SemaphoreType.DMA((11, steps)),
            pltpu.SemaphoreType.DMA((11, steps)),
        ],
        compiler_params=pltpu.CompilerParams(
            collective_id=0, has_side_effects=True, vmem_limit_bytes=56 * 2**20
        ),
    )(tokens, expert_ids.T, gate_scales.T, w_gate, w_up, w_down)


def body(tokens, expert_ids, gate_scales, w_gate, w_up, w_down):
    rows, top_k = expert_ids.shape
    sources = lax.axis_size("expert")
    experts_all = w_gate.shape[0] * sources
    every_slot_used = 2 * rows * top_k // experts_all >= rows
    grouped = w_gate.shape[0] == 2 and lax.axis_size("dp") == 4 and sources == 8
    chosen = dense_body if every_slot_used and grouped else routed_body
    return chosen(tokens, expert_ids, gate_scales, w_gate, w_up, w_down)


def solution(mesh):
    in_specs = (
        P("expert", "dp"),
        P("expert", None),
        P("expert", None),
        P("expert", "dp", None),
        P("expert", "dp", None),
        P("expert", None, "dp"),
    )
    out_specs = P("expert", "dp")
    return jax.shard_map(body, mesh=mesh, in_specs=in_specs, out_specs=out_specs, check_vma=False)
```

```python
import functools

import jax
import jax.numpy as jnp
from jax import lax
from jax.experimental import pallas as pl
from jax.experimental.pallas import tpu as pltpu
from jax.sharding import PartitionSpec as P


def running_count(hits):
    count = hits.shape[-2]
    upto = jnp.tril(jnp.ones((count, count), jnp.bfloat16))
    sums = jnp.einsum("ij,...jm->...im", upto, hits.astype(jnp.bfloat16), preferred_element_type=jnp.float32)
    return sums.astype(jnp.int32)


def routed_body(tokens, expert_ids, gate_scales, w_gate, w_up, w_down):
    tok_rows, slice_width = tokens.shape
    top_k = expert_ids.shape[1]
    source_count = lax.axis_size("expert")
    local_experts = w_gate.shape[0]
    hidden_units = w_gate.shape[2]
    experts_all = local_experts * source_count
    capacity = 2 * tok_rows * top_k // experts_all
    assigns = tok_rows * top_k
    owner_rows = source_count * capacity
    flat_ids = expert_ids.reshape(assigns)
    catalog = jnp.arange(experts_all, dtype=jnp.int32)
    onehot = (flat_ids[:, None] == catalog[None, :]).astype(jnp.int32)
    rank_in = jnp.sum((running_count(onehot) - 1) * onehot, axis=1)
    owners = flat_ids // local_experts
    within = flat_ids % local_experts
    slot_index = within * owner_rows + owners * capacity + rank_in
    every_token = lax.all_gather(tokens, "expert", axis=0, tiled=True)
    every_id = lax.all_gather(expert_ids, "expert", axis=0, tiled=True)
    my_index = lax.axis_index("expert")
    grouped = every_id.reshape(source_count, assigns) - my_index * local_experts
    my_hits = (
        grouped[:, :, None] == jnp.arange(local_experts, dtype=jnp.int32)[None, None, :]
    ).astype(jnp.int32)
    my_ranks = jnp.sum((running_count(my_hits) - 1) * my_hits, axis=2)
    hit_count = jnp.sum(my_hits, axis=2)
    sources = jnp.arange(source_count, dtype=jnp.int32)[:, None]
    target = jnp.where(
        hit_count > 0,
        grouped * owner_rows + sources * capacity + my_ranks,
        local_experts * owner_rows,
    )
    anchor = sources * tok_rows + jnp.arange(assigns, dtype=jnp.int32)[None, :] // top_k
    token_total = source_count * tok_rows
    lookup = (
        jnp.full((local_experts * owner_rows,), token_total, jnp.int32)
        .at[target.reshape(-1)]
        .set(anchor.reshape(-1), mode="drop")
    )
    padded = jnp.concatenate([every_token, jnp.zeros((1, slice_width), tokens.dtype)], axis=0)
    arrived = padded[lookup].reshape(local_experts, owner_rows, slice_width)
    outputs = []
    for local_index in range(local_experts):
        rows_here = arrived[local_index]
        gate_here = w_gate[local_index]
        up_here = w_up[local_index]
        down_here = w_down[local_index]
        gate_part = jnp.dot(rows_here, gate_here, preferred_element_type=jnp.float32)
        up_part = jnp.dot(rows_here, up_here, preferred_element_type=jnp.float32)
        summed = lax.psum_scatter(
            jnp.concatenate([gate_part, up_part], axis=1).astype(jnp.bfloat16),
            "dp",
            scatter_dimension=0,
            tiled=True,
        ).astype(jnp.float32)
        hidden = (jax.nn.silu(summed[:, :hidden_units]) * summed[:, hidden_units:]).astype(
            jnp.bfloat16
        )
        outputs.append(
            jnp.dot(
                lax.all_gather(hidden, "dp", axis=0, tiled=True),
                down_here,
                preferred_element_type=jnp.float32,
            ).astype(jnp.bfloat16)
        )
    results = jnp.stack(outputs).reshape(local_experts, source_count, capacity, slice_width)
    returned = lax.all_to_all(results, "expert", split_axis=1, concat_axis=1, tiled=True)
    returned = returned.reshape(local_experts * owner_rows, slice_width)
    picked = returned[slot_index].reshape(tok_rows, top_k, slice_width)
    mixed = jnp.sum(gate_scales[:, :, None] * picked.astype(jnp.float32), axis=1)
    return mixed.astype(jnp.bfloat16)


MESH = pl.DeviceIdType.MESH
(
    CORE, ACROSS, HIDDEN_ACROSS, HIDDEN_CORE, HIDDEN_FORWARD, TOKEN_LINE, TOKEN_PAIR,
    SCALE_LINE, SCALE_PAIR, RESULT_PAIR, RESULT_LINE,
) = range(11)

ORDER = (
    (0, 0, 0), (0, 1, 0),
    (1, 0, 0), (1, 1, 0), (1, 0, 1), (1, 1, 1),
    (2, 0, 0), (2, 0, 1), (2, 1, 0), (2, 1, 1),
    (3, 1, 0), (3, 1, 1), (3, 0, 0), (3, 0, 1),
    (0, 1, 1), (0, 0, 1),
)
RELAY = {2: ((1, 0),), 4: ((1, 1),), 6: ((2, 0),), 7: ((2, 1),), 8: ((3, 0),), 9: ((3, 1),)}
SEND = {1: ((1, 1),), 3: ((2, 0),), 4: ((2, 1),), 6: ((3, 0),), 7: ((3, 1),)}
LATE_PAIR = 9
MERGE_AT = 12
MERGE = ((1, 0), (1, 1), (2, 0), (2, 1), (3, 0), (3, 1))


def pick(index, table):
    value = jnp.int32(table[0])
    for place in range(1, len(table)):
        value = jnp.where(index >= place, jnp.int32(table[place]), value)
    return value


def peer_of(me, step):
    total = 0
    for bit in (1, 2, 4):
        total = total + bit * ((me // bit + step // bit) % 2)
    return total


def chunk_at(step):
    code = pick(step, [away * 4 + pair * 2 + part for away, pair, part in ORDER])
    return code // 4, code // 2 % 2, code % 2


def dense_kernel(
    tokens, ids, scales, w_gate, w_up, w_down, out,
    ids_v, scales_v, out_v, first_half, tok_buf, gate_v, up_v, down_v, scale_buf,
    core_send, core_recv, kept_part, across_send, across_recv, kept_sum,
    hidden, kept_result, pair_send, pair_recv, line_send, line_recv, weight_sem, send_sem, recv_sem,
):
    me = lax.axis_index("expert")
    slice_index = lax.axis_index("dp")
    core = slice_index % 2
    side = slice_index // 2
    other_core, other_side = 1 - core, 1 - side
    core_device = (me, side * 2 + other_core)
    side_device = (me, other_side * 2 + core)
    rows, width = tokens.shape
    part_rows = rows // 2
    half = hidden.shape[-1]
    line, steps = tok_buf.shape[0], core_send.shape[0]
    experts = scale_buf.shape[2]

    pair_device = (peer_of(me, 1), slice_index)

    def line_device(away):
        return (peer_of(me, 2 * away), slice_index)

    barrier = pltpu.get_barrier_semaphore()
    greeted = [core_device, side_device, pair_device] + [line_device(away) for away in range(1, line)]
    for device in greeted:
        pl.semaphore_signal(barrier, inc=1, device_id=device, device_id_type=MESH)

    def load(place, source, target):
        return pltpu.make_async_copy(source, target, weight_sem.at[place])

    loads = [
        load(0, w_gate.at[other_core], gate_v.at[other_core]),
        load(1, w_up.at[other_core], up_v.at[other_core]),
        load(2, w_gate.at[core], gate_v.at[core]),
        load(3, w_up.at[core], up_v.at[core]),
        load(4, w_down, down_v),
    ]
    small = [
        load(5, ids, ids_v),
        load(6, scales, scales_v),
        load(7, tokens.at[0:part_rows], tok_buf.at[0, 0, 0]),
        load(8, tokens.at[part_rows:rows], tok_buf.at[0, 0, 1]),
    ]
    for each in small + loads:
        each.start()
    for each in small:
        each.wait()
    which_expert = lax.broadcasted_iota(jnp.int32, (experts, rows), 0)
    table = jnp.zeros((experts, rows), jnp.float32)
    for k in range(ids_v.shape[0]):
        table = table + jnp.where(which_expert == ids_v[k : k + 1, :], scales_v[k : k + 1, :], 0.0)
    scale_buf[0, 0] = table

    pl.semaphore_wait(barrier, len(greeted))

    def copy(kind, step, source, target, device):
        return pltpu.make_async_remote_copy(
            src_ref=source,
            dst_ref=target,
            send_sem=send_sem.at[kind, step],
            recv_sem=recv_sem.at[kind, step],
            device_id=device,
            device_id_type=MESH,
        )

    def line_token(away, part):
        return copy(
            TOKEN_LINE, away * 2 + part, tok_buf.at[0, 0, part], tok_buf.at[away, 0, part], line_device(away)
        )

    def pair_token(away, part):
        return copy(
            TOKEN_PAIR, away * 2 + part, tok_buf.at[away, 0, part], tok_buf.at[away, 1, part], pair_device
        )

    def line_scale(away):
        return copy(SCALE_LINE, away, scale_buf.at[0, 0], scale_buf.at[away, 0], line_device(away))

    def pair_scale(away):
        return copy(SCALE_PAIR, away, scale_buf.at[away, 0], scale_buf.at[away, 1], pair_device)

    def core_copy(step):
        return copy(CORE, step, core_send.at[step], core_recv.at[step], core_device)

    def across_copy(step):
        return copy(ACROSS, step, across_send.at[step], across_recv.at[step], side_device)

    def hidden_copy(kind, step, owner, part, device):
        piece = hidden.at[step, owner, part]
        return copy(kind, step, piece, piece, device)

    middle = width // 256 * 128
    columns = (pl.ds(0, middle), pl.ds(middle, width - middle))

    def pair_result(away, part, piece):
        where = (away, part, slice(None), columns[piece])
        return copy(
            RESULT_PAIR, (away * 2 + part) * 2 + piece, pair_send.at[where], pair_recv.at[where], pair_device
        )

    def line_result(away, part):
        return copy(
            RESULT_LINE, away * 2 + part, line_send.at[away, part], line_recv.at[away, part], line_device(away)
        )

    pair_token(0, 0).start()
    line_token(1, 0).start()
    pair_scale(0).start()
    for away in range(1, line):
        line_scale(away).start()

    def project_other(step, block):
        for which, weights in enumerate((gate_v, up_v)):
            for cut in range(2):
                core_send[step, which, cut] = jnp.dot(
                    block, weights[other_core, :, cut * half : (cut + 1) * half],
                    preferred_element_type=jnp.float32,
                ).astype(jnp.bfloat16)
        core_copy(step).start()

    def project_own(step, block):
        for which, weights in enumerate((gate_v, up_v)):
            for cut in range(2):
                kept_part[step % 2, which, cut] = jnp.dot(
                    block, weights[core, :, cut * half : (cut + 1) * half],
                    preferred_element_type=jnp.float32,
                )

    def project(step):
        away, pair, part = chunk_at(step)

        @pl.when(pair == 1)
        def _():
            pair_token(away, part).wait_recv()

        block = tok_buf[away, pair, part]
        project_other(step, block)
        project_own(step, block)

    def add_core(step):
        core_copy(step).wait_recv()
        slot = step % 2
        for which in range(2):
            across_send[step, which] = (
                kept_part[slot, which, other_side]
                + core_recv[step, which, other_side].astype(jnp.float32)
            ).astype(jnp.bfloat16)
        across_copy(step).start()
        for which in range(2):
            kept_sum[step % 3, which] = kept_part[slot, which, side] + core_recv[
                step, which, side
            ].astype(jnp.float32)

    def activate(step):
        away, pair, part = chunk_at(step)

        @pl.when((part == 0) & (pair == 1))
        def _():
            pair_scale(away).wait_recv()

        across_copy(step).wait_recv()
        slot = step % 3
        shape = (part_rows, rows)
        chosen = lax.broadcasted_iota(jnp.int32, shape, 0) + part * part_rows == (
            lax.broadcasted_iota(jnp.int32, shape, 1)
        )
        row = scale_buf[away, pair, pl.ds(2 * me + core, 1), :]
        scale = jnp.sum(jnp.where(chosen, row, 0.0), axis=1, keepdims=True)
        gate = kept_sum[slot, 0] + across_recv[step, 0].astype(jnp.float32)
        up = kept_sum[slot, 1] + across_recv[step, 1].astype(jnp.float32)
        hidden[step, core, side] = (gate / (1.0 + jnp.exp(-gate)) * up * scale).astype(jnp.bfloat16)
        hidden_copy(HIDDEN_ACROSS, step, core, side, side_device).start()
        hidden_copy(HIDDEN_CORE, step, core, side, core_device).start()

    def forward(step):
        hidden_copy(HIDDEN_ACROSS, step, core, other_side, side_device).wait_recv()
        hidden_copy(HIDDEN_FORWARD, step, core, other_side, core_device).start()

    def finish(step):
        away, pair, part = chunk_at(step)

        @pl.when(step == 0)
        def _():
            loads[4].wait()

        def share(cut, piece):
            low = pl.multiple_of(cut * half, half)
            return sum(
                jnp.dot(
                    hidden[step, owner, cut], down_v[owner, pl.ds(low, half), columns[piece]],
                    preferred_element_type=jnp.float32,
                )
                for owner in range(2)
            )

        hidden_copy(HIDDEN_CORE, step, other_core, side, core_device).wait_recv()
        for piece in range(2):
            first_half[:, columns[piece]] = share(side, piece)
        hidden_copy(HIDDEN_FORWARD, step, other_core, other_side, core_device).wait_recv()
        for piece in range(2):
            value = first_half[:, columns[piece]] + share(other_side, piece)

            @pl.when(pair == 0)
            def _():
                kept_result[away, part, :, columns[piece]] = value

            @pl.when(pair == 1)
            def _():
                pair_send[away, part, :, columns[piece]] = value.astype(jnp.bfloat16)
                pair_result(away, part, piece).start()

    def merge(place):
        away, part = pick(place, [entry[0] for entry in MERGE]), place % 2
        for piece in range(2):
            pair_result(away, part, piece).wait_recv()
        line_send[away, part] = (
            kept_result[away, part] + pair_recv[away, part].astype(jnp.float32)
        ).astype(jnp.bfloat16)
        line_result(away, part).start()

    def store(part):
        rows_here = pl.ds(part * part_rows, part_rows)
        return pltpu.make_async_copy(out_v.at[rows_here], out.at[rows_here], weight_sem.at[9 + part])

    def conclude(part):
        for piece in range(2):
            pair_result(0, part, piece).wait_recv()
        value = kept_result[0, part] + pair_recv[0, part].astype(jnp.float32)
        for away in (2, 3, 1):
            line_result(away, part).wait_recv()
            value = value + line_recv[away, part].astype(jnp.float32)
        rows_here = pl.ds(part * part_rows, part_rows)
        out_v[rows_here] = value.astype(out_v.dtype)
        store(part).start()

    loads[0].wait()
    loads[1].wait()
    project_other(0, tok_buf[0, 0, 0])
    loads[2].wait()
    loads[3].wait()
    project_own(0, tok_buf[0, 0, 0])

    def staged(turn, lag, stage):
        @pl.when((turn >= lag) & (turn < steps + lag))
        def _():
            stage(turn - lag)

    def iteration(turn, carry):
        staged(turn, 1, add_core)
        for at, entries in RELAY.items():
            @pl.when(turn == at)
            def _():
                for away, part in entries:
                    line_token(away, part).wait_recv()
                    pair_token(away, part).start()
                    if part == 0:
                        line_scale(away).wait_recv()
                        pair_scale(away).start()
        for at, entries in SEND.items():
            @pl.when(turn == at)
            def _():
                for away, part in entries:
                    line_token(away, part).start()

        @pl.when(turn == LATE_PAIR)
        def _():
            pair_token(0, 1).start()

        staged(turn, 0, project)
        @pl.when(turn == steps + 3)
        def _():
            conclude(0)

        staged(turn, 4, finish)
        @pl.when((turn >= MERGE_AT) & (turn < MERGE_AT + len(MERGE)))
        def _():
            merge(turn - MERGE_AT)

        staged(turn, 2, activate)
        staged(turn, 3, forward)

        return carry

    lax.fori_loop(1, steps + 4, iteration, 0)

    conclude(1)

    def drain(step, carry):
        core_copy(step).wait_send()
        across_copy(step).wait_send()
        hidden_copy(HIDDEN_ACROSS, step, core, side, side_device).wait_send()
        hidden_copy(HIDDEN_CORE, step, core, side, core_device).wait_send()
        hidden_copy(HIDDEN_FORWARD, step, core, other_side, core_device).wait_send()
        return carry

    lax.fori_loop(0, steps, drain, 0)
    for part in range(2):
        store(part).wait()
    for away in range(line):
        pair_scale(away).wait_send()
        if away > 0:
            line_scale(away).wait_send()
        for part in range(2):
            pair_token(away, part).wait_send()
            for piece in range(2):
                pair_result(away, part, piece).wait_send()
            if away > 0:
                line_token(away, part).wait_send()
                line_result(away, part).wait_send()


def dense_body(tokens, expert_ids, gate_scales, w_gate, w_up, w_down):
    rows, width = tokens.shape
    sources = lax.axis_size("expert")
    line, steps, part_rows = sources // 2, 2 * sources, rows // 2
    experts = w_gate.shape[0] * sources
    half = w_gate.shape[2] // 2
    narrow, wide = jnp.bfloat16, jnp.float32
    top_k = expert_ids.shape[1]
    anywhere = pl.BlockSpec(memory_space=pl.ANY)
    return pl.pallas_call(
        dense_kernel,
        out_shape=jax.ShapeDtypeStruct((rows, width), narrow),
        in_specs=[anywhere] * 6,
        out_specs=anywhere,
        scratch_shapes=[
            pltpu.VMEM((top_k, rows), jnp.int32),
            pltpu.VMEM((top_k, rows), wide),
            pltpu.VMEM((rows, width), narrow),
            pltpu.VMEM((part_rows, width), wide),
            pltpu.VMEM((line, 2, 2, part_rows, width), narrow),
            pltpu.VMEM(w_gate.shape, narrow),
            pltpu.VMEM(w_up.shape, narrow),
            pltpu.VMEM(w_down.shape, narrow),
            pltpu.VMEM((line, 2, experts, rows), wide),
            pltpu.VMEM((steps, 2, 2, part_rows, half), narrow),
            pltpu.VMEM((steps, 2, 2, part_rows, half), narrow),
            pltpu.VMEM((2, 2, 2, part_rows, half), wide),
            pltpu.VMEM((steps, 2, part_rows, half), narrow),
            pltpu.VMEM((steps, 2, part_rows, half), narrow),
            pltpu.VMEM((3, 2, part_rows, half), wide),
            pltpu.VMEM((steps, 2, 2, part_rows, half), narrow),
            pltpu.VMEM((line, 2, part_rows, width), wide),
            pltpu.VMEM((line, 2, part_rows, width), narrow),
            pltpu.VMEM((line, 2, part_rows, width), narrow),
            pltpu.VMEM((line, 2, part_rows, width), narrow),
            pltpu.VMEM((line, 2, part_rows, width), narrow),
            pltpu.SemaphoreType.DMA((11,)),
            pltpu.SemaphoreType.DMA((11, steps)),
            pltpu.SemaphoreType.DMA((11, steps)),
        ],
        compiler_params=pltpu.CompilerParams(
            collective_id=0, has_side_effects=True, vmem_limit_bytes=56 * 2**20
        ),
    )(tokens, expert_ids.T, gate_scales.T, w_gate, w_up, w_down)


def body(tokens, expert_ids, gate_scales, w_gate, w_up, w_down):
    rows, top_k = expert_ids.shape
    sources = lax.axis_size("expert")
    experts_all = w_gate.shape[0] * sources
    every_slot_used = 2 * rows * top_k // experts_all >= rows
    grouped = w_gate.shape[0] == 2 and lax.axis_size("dp") == 4 and sources == 8
    chosen = dense_body if every_slot_used and grouped else routed_body
    return chosen(tokens, expert_ids, gate_scales, w_gate, w_up, w_down)


def solution(mesh):
    in_specs = (
        P("expert", "dp"),
        P("expert", None),
        P("expert", None),
        P("expert", "dp", None),
        P("expert", "dp", None),
        P("expert", None, "dp"),
    )
    out_specs = P("expert", "dp")
    return jax.shard_map(body, mesh=mesh, in_specs=in_specs, out_specs=out_specs, check_vma=False)
```

```python
import functools

import jax
import jax.numpy as jnp
from jax import lax
from jax.experimental import pallas as pl
from jax.experimental.pallas import tpu as pltpu
from jax.sharding import PartitionSpec as P


def running_count(hits):
    count = hits.shape[-2]
    upto = jnp.tril(jnp.ones((count, count), jnp.bfloat16))
    sums = jnp.einsum("ij,...jm->...im", upto, hits.astype(jnp.bfloat16), preferred_element_type=jnp.float32)
    return sums.astype(jnp.int32)


def routed_body(tokens, expert_ids, gate_scales, w_gate, w_up, w_down):
    tok_rows, slice_width = tokens.shape
    top_k = expert_ids.shape[1]
    source_count = lax.axis_size("expert")
    local_experts = w_gate.shape[0]
    hidden_units = w_gate.shape[2]
    experts_all = local_experts * source_count
    capacity = 2 * tok_rows * top_k // experts_all
    assigns = tok_rows * top_k
    owner_rows = source_count * capacity
    flat_ids = expert_ids.reshape(assigns)
    catalog = jnp.arange(experts_all, dtype=jnp.int32)
    onehot = (flat_ids[:, None] == catalog[None, :]).astype(jnp.int32)
    rank_in = jnp.sum((running_count(onehot) - 1) * onehot, axis=1)
    owners = flat_ids // local_experts
    within = flat_ids % local_experts
    slot_index = within * owner_rows + owners * capacity + rank_in
    every_token = lax.all_gather(tokens, "expert", axis=0, tiled=True)
    every_id = lax.all_gather(expert_ids, "expert", axis=0, tiled=True)
    my_index = lax.axis_index("expert")
    grouped = every_id.reshape(source_count, assigns) - my_index * local_experts
    my_hits = (
        grouped[:, :, None] == jnp.arange(local_experts, dtype=jnp.int32)[None, None, :]
    ).astype(jnp.int32)
    my_ranks = jnp.sum((running_count(my_hits) - 1) * my_hits, axis=2)
    hit_count = jnp.sum(my_hits, axis=2)
    sources = jnp.arange(source_count, dtype=jnp.int32)[:, None]
    target = jnp.where(
        hit_count > 0,
        grouped * owner_rows + sources * capacity + my_ranks,
        local_experts * owner_rows,
    )
    anchor = sources * tok_rows + jnp.arange(assigns, dtype=jnp.int32)[None, :] // top_k
    token_total = source_count * tok_rows
    lookup = (
        jnp.full((local_experts * owner_rows,), token_total, jnp.int32)
        .at[target.reshape(-1)]
        .set(anchor.reshape(-1), mode="drop")
    )
    padded = jnp.concatenate([every_token, jnp.zeros((1, slice_width), tokens.dtype)], axis=0)
    arrived = padded[lookup].reshape(local_experts, owner_rows, slice_width)
    outputs = []
    for local_index in range(local_experts):
        rows_here = arrived[local_index]
        gate_here = w_gate[local_index]
        up_here = w_up[local_index]
        down_here = w_down[local_index]
        gate_part = jnp.dot(rows_here, gate_here, preferred_element_type=jnp.float32)
        up_part = jnp.dot(rows_here, up_here, preferred_element_type=jnp.float32)
        summed = lax.psum_scatter(
            jnp.concatenate([gate_part, up_part], axis=1).astype(jnp.bfloat16),
            "dp",
            scatter_dimension=0,
            tiled=True,
        ).astype(jnp.float32)
        hidden = (jax.nn.silu(summed[:, :hidden_units]) * summed[:, hidden_units:]).astype(
            jnp.bfloat16
        )
        outputs.append(
            jnp.dot(
                lax.all_gather(hidden, "dp", axis=0, tiled=True),
                down_here,
                preferred_element_type=jnp.float32,
            ).astype(jnp.bfloat16)
        )
    results = jnp.stack(outputs).reshape(local_experts, source_count, capacity, slice_width)
    returned = lax.all_to_all(results, "expert", split_axis=1, concat_axis=1, tiled=True)
    returned = returned.reshape(local_experts * owner_rows, slice_width)
    picked = returned[slot_index].reshape(tok_rows, top_k, slice_width)
    mixed = jnp.sum(gate_scales[:, :, None] * picked.astype(jnp.float32), axis=1)
    return mixed.astype(jnp.bfloat16)


MESH = pl.DeviceIdType.MESH
(
    CORE, ACROSS, HIDDEN_ACROSS, HIDDEN_CORE, HIDDEN_FORWARD, TOKEN_LINE, TOKEN_PAIR,
    SCALE_LINE, SCALE_PAIR, RESULT_PAIR, RESULT_LINE,
) = range(11)

ORDER = ((0, 0, 0), (0, 1, 0), (1, 0, 0), (1, 1, 0), (1, 1, 1), (2, 0, 0), (2, 1, 0), (2, 0, 1), (2, 1, 1), (3, 1, 0), (3, 0, 0), (3, 1, 1), (3, 0, 1), (1, 0, 1), (0, 1, 1), (0, 0, 1))
RELAY = {2: ((1, 0),), 3: ((1, 1),), 5: ((2, 0),), 7: ((2, 1),), 8: ((3, 0),), 10: ((3, 1),)}
SEND = {1: ((1, 1),), 3: ((2, 0),), 4: ((2, 1),), 6: ((3, 0),), 7: ((3, 1),)}
LATE_PAIR = 9
MERGE_AT = 12
MERGE = ((2, 0), (2, 1), (3, 0), (1, 0), (3, 1), (1, 1))


def pick(index, table):
    value = jnp.int32(table[0])
    for place in range(1, len(table)):
        value = jnp.where(index >= place, jnp.int32(table[place]), value)
    return value


def peer_of(me, step):
    total = 0
    for bit in (1, 2, 4):
        total = total + bit * ((me // bit + step // bit) % 2)
    return total


def chunk_at(step):
    code = pick(step, [away * 4 + pair * 2 + part for away, pair, part in ORDER])
    return code // 4, code // 2 % 2, code % 2


def dense_kernel(
    tokens, ids, scales, w_gate, w_up, w_down, out,
    ids_v, scales_v, out_v, first_half, tok_buf, gate_v, up_v, down_v, scale_buf,
    core_send, core_recv, kept_part, across_send, across_recv, kept_sum,
    hidden, kept_result, pair_send, pair_recv, line_send, line_recv, weight_sem, line_ready, send_sem, recv_sem,
):
    me = lax.axis_index("expert")
    slice_index = lax.axis_index("dp")
    core = slice_index % 2
    side = slice_index // 2
    other_core, other_side = 1 - core, 1 - side
    core_device = (me, side * 2 + other_core)
    side_device = (me, other_side * 2 + core)
    rows, width = tokens.shape
    part_rows = rows // 2
    half = hidden.shape[-1]
    line, steps = tok_buf.shape[0], core_send.shape[0]
    experts = scale_buf.shape[2]

    pair_device = (peer_of(me, 1), slice_index)

    def line_device(away):
        return (peer_of(me, 2 * away), slice_index)

    barrier = pltpu.get_barrier_semaphore()
    place = me // 2
    inner = (place == 1) | (place == 2)
    greeted = [core_device, side_device, pair_device, line_device(1)]
    for device in greeted:
        pl.semaphore_signal(barrier, inc=1, device_id=device, device_id_type=MESH)

    @pl.when(inner)
    def _():
        pl.semaphore_signal(barrier, inc=1, device_id=line_device(3), device_id_type=MESH)


    def load(place, source, target):
        return pltpu.make_async_copy(source, target, weight_sem.at[place])

    loads = [
        load(0, w_gate.at[other_core], gate_v.at[other_core]),
        load(1, w_up.at[other_core], up_v.at[other_core]),
        load(2, w_gate.at[core], gate_v.at[core]),
        load(3, w_up.at[core], up_v.at[core]),
        load(4, w_down, down_v),
    ]
    small = [
        load(5, tokens.at[0:part_rows], tok_buf.at[0, 0, 0]),
        load(6, tokens.at[part_rows:rows], tok_buf.at[0, 0, 1]),
        load(7, ids, ids_v),
        load(8, scales, scales_v),
    ]
    for each in small + loads:
        each.start()
    small[0].wait()
    @pl.when(inner)
    def _():
        pl.semaphore_wait(barrier, len(greeted) + 1)

    @pl.when(jnp.logical_not(inner))
    def _():
        pl.semaphore_wait(barrier, len(greeted))

    @pl.when(inner)
    def _():
        pl.semaphore_signal(line_ready, inc=1, device_id=line_device(3), device_id_type=MESH)


    def copy(kind, step, source, target, device):
        return pltpu.make_async_remote_copy(
            src_ref=source,
            dst_ref=target,
            send_sem=send_sem.at[kind, step],
            recv_sem=recv_sem.at[kind, step],
            device_id=device,
            device_id_type=MESH,
        )

    def line_token(away, part):
        return copy(
            TOKEN_LINE, away * 2 + part, tok_buf.at[0, 0, part], tok_buf.at[away, 0, part], line_device(away)
        )

    def pair_token(away, part):
        return copy(
            TOKEN_PAIR, away * 2 + part, tok_buf.at[away, 0, part], tok_buf.at[away, 1, part], pair_device
        )

    def line_scale(away):
        return copy(SCALE_LINE, away, scale_buf.at[0, 0], scale_buf.at[away, 0], line_device(away))

    def pair_scale(away):
        return copy(SCALE_PAIR, away, scale_buf.at[away, 0], scale_buf.at[away, 1], pair_device)

    def core_copy(step):
        return copy(CORE, step, core_send.at[step], core_recv.at[step], core_device)

    def across_copy(step):
        return copy(ACROSS, step, across_send.at[step], across_recv.at[step], side_device)

    def hidden_copy(kind, step, owner, part, device):
        piece = hidden.at[step, owner, part]
        return copy(kind, step, piece, piece, device)

    middle = width // 256 * 128
    columns = (pl.ds(0, middle), pl.ds(middle, width - middle))

    def pair_result(away, part, piece):
        where = (away, part, slice(None), columns[piece])
        return copy(
            RESULT_PAIR, (away * 2 + part) * 2 + piece, pair_send.at[where], pair_recv.at[where], pair_device
        )

    def line_result(away, part):
        return copy(
            RESULT_LINE, away * 2 + part, line_send.at[away, part], line_recv.at[away, part], line_device(away)
        )

    pair_token(0, 0).start()
    line_token(1, 0).start()

    def project_other(step, block):
        for which, weights in enumerate((gate_v, up_v)):
            for cut in range(2):
                core_send[step, which, cut] = jnp.dot(
                    block, weights[other_core, :, cut * half : (cut + 1) * half],
                    preferred_element_type=jnp.float32,
                ).astype(jnp.bfloat16)
        core_copy(step).start()

    def project_own(step, block):
        for which, weights in enumerate((gate_v, up_v)):
            for cut in range(2):
                kept_part[step % 2, which, cut] = jnp.dot(
                    block, weights[core, :, cut * half : (cut + 1) * half],
                    preferred_element_type=jnp.float32,
                )

    def project(step):
        away, pair, part = chunk_at(step)

        @pl.when(pair == 1)
        def _():
            pair_token(away, part).wait_recv()

        block = tok_buf[away, pair, part]
        project_other(step, block)
        project_own(step, block)

    def add_core(step):
        core_copy(step).wait_recv()
        slot = step % 2
        for which in range(2):
            across_send[step, which] = (
                kept_part[slot, which, other_side]
                + core_recv[step, which, other_side].astype(jnp.float32)
            ).astype(jnp.bfloat16)
        across_copy(step).start()
        for which in range(2):
            kept_sum[step % 3, which] = kept_part[slot, which, side] + core_recv[
                step, which, side
            ].astype(jnp.float32)

    def activate(step):
        away, pair, part = chunk_at(step)

        @pl.when((part == 0) & (pair == 1))
        def _():
            pair_scale(away).wait_recv()

        across_copy(step).wait_recv()
        slot = step % 3
        shape = (part_rows, rows)
        chosen = lax.broadcasted_iota(jnp.int32, shape, 0) + part * part_rows == (
            lax.broadcasted_iota(jnp.int32, shape, 1)
        )
        row = scale_buf[away, pair, pl.ds(2 * me + core, 1), :]
        scale = jnp.sum(jnp.where(chosen, row, 0.0), axis=1, keepdims=True)
        gate = kept_sum[slot, 0] + across_recv[step, 0].astype(jnp.float32)
        up = kept_sum[slot, 1] + across_recv[step, 1].astype(jnp.float32)
        hidden[step, core, side] = (gate / (1.0 + jnp.exp(-gate)) * up * scale).astype(jnp.bfloat16)
        hidden_copy(HIDDEN_ACROSS, step, core, side, side_device).start()
        hidden_copy(HIDDEN_CORE, step, core, side, core_device).start()

    def forward(step):
        hidden_copy(HIDDEN_ACROSS, step, core, other_side, side_device).wait_recv()
        hidden_copy(HIDDEN_FORWARD, step, core, other_side, core_device).start()

    def finish(step):
        away, pair, part = chunk_at(step)

        @pl.when(step == 0)
        def _():
            loads[4].wait()

        def share(cut, piece):
            low = pl.multiple_of(cut * half, half)
            return sum(
                jnp.dot(
                    hidden[step, owner, cut], down_v[owner, pl.ds(low, half), columns[piece]],
                    preferred_element_type=jnp.float32,
                )
                for owner in range(2)
            )

        hidden_copy(HIDDEN_CORE, step, other_core, side, core_device).wait_recv()
        for piece in range(2):
            first_half[:, columns[piece]] = share(side, piece)
        hidden_copy(HIDDEN_FORWARD, step, other_core, other_side, core_device).wait_recv()
        for piece in range(2):
            value = first_half[:, columns[piece]] + share(other_side, piece)

            @pl.when(pair == 0)
            def _():
                kept_result[away, part, :, columns[piece]] = value

            @pl.when(pair == 1)
            def _():
                pair_send[away, part, :, columns[piece]] = value.astype(jnp.bfloat16)
                pair_result(away, part, piece).start()

    def merge(place):
        away, part = pick(place, [entry[0] for entry in MERGE]), pick(place, [entry[1] for entry in MERGE])
        for piece in range(2):
            pair_result(away, part, piece).wait_recv()
        line_send[away, part] = (
            kept_result[away, part] + pair_recv[away, part].astype(jnp.float32)
        ).astype(jnp.bfloat16)
        line_result(away, part).start()

    def store(part):
        rows_here = pl.ds(part * part_rows, part_rows)
        return pltpu.make_async_copy(out_v.at[rows_here], out.at[rows_here], weight_sem.at[9 + part])

    def conclude(part):
        for piece in range(2):
            pair_result(0, part, piece).wait_recv()
        value = kept_result[0, part] + pair_recv[0, part].astype(jnp.float32)
        for away in (2, 3, 1):
            line_result(away, part).wait_recv()
            value = value + line_recv[away, part].astype(jnp.float32)
        rows_here = pl.ds(part * part_rows, part_rows)
        out_v[rows_here] = value.astype(out_v.dtype)
        store(part).start()

    loads[0].wait()
    loads[1].wait()
    project_other(0, tok_buf[0, 0, 0])
    loads[2].wait()
    loads[3].wait()
    project_own(0, tok_buf[0, 0, 0])
    for each in small[1:]:
        each.wait()
    which_expert = lax.broadcasted_iota(jnp.int32, (experts, rows), 0)
    table = jnp.zeros((experts, rows), jnp.float32)
    for k in range(ids_v.shape[0]):
        table = table + jnp.where(which_expert == ids_v[k : k + 1, :], scales_v[k : k + 1, :], 0.0)
    scale_buf[0, 0] = table
    pair_scale(0).start()
    line_scale(1).start()

    def staged(turn, lag, stage):
        @pl.when((turn >= lag) & (turn < steps + lag))
        def _():
            stage(turn - lag)

    def iteration(turn, carry):
        staged(turn, 1, add_core)
        for at, entries in RELAY.items():
            @pl.when(turn == at)
            def _():
                for away, part in entries:
                    line_token(away, part).wait_recv()
                    pair_token(away, part).start()
                    if part == 0:
                        line_scale(away).wait_recv()
                        pair_scale(away).start()
        @pl.when((turn == 2) & inner)
        def _():
            pl.semaphore_wait(line_ready, 1)
            pl.semaphore_signal(line_ready, inc=1, device_id=line_device(1), device_id_type=MESH)

        @pl.when((turn == 3) & jnp.logical_not(inner))
        def _():
            pl.semaphore_wait(line_ready, 1)

        for at, entries in SEND.items():
            @pl.when(turn == at)
            def _():
                for away, part in entries:
                    if away > 1 and part == 0:
                        line_scale(away).start()
                    line_token(away, part).start()

        @pl.when(turn == LATE_PAIR)
        def _():
            pair_token(0, 1).start()

        staged(turn, 0, project)
        @pl.when(turn == steps + 3)
        def _():
            conclude(0)

        staged(turn, 4, finish)
        @pl.when((turn >= MERGE_AT) & (turn < MERGE_AT + len(MERGE)))
        def _():
            merge(turn - MERGE_AT)

        staged(turn, 2, activate)
        staged(turn, 3, forward)

        return carry

    lax.fori_loop(1, steps + 4, iteration, 0)

    conclude(1)

    def drain(step, carry):
        core_copy(step).wait_send()
        across_copy(step).wait_send()
        hidden_copy(HIDDEN_ACROSS, step, core, side, side_device).wait_send()
        hidden_copy(HIDDEN_CORE, step, core, side, core_device).wait_send()
        hidden_copy(HIDDEN_FORWARD, step, core, other_side, core_device).wait_send()
        return carry

    lax.fori_loop(0, steps, drain, 0)
    for part in range(2):
        store(part).wait()
    for away in range(line):
        pair_scale(away).wait_send()
        if away > 0:
            line_scale(away).wait_send()
        for part in range(2):
            pair_token(away, part).wait_send()
            for piece in range(2):
                pair_result(away, part, piece).wait_send()
            if away > 0:
                line_token(away, part).wait_send()
                line_result(away, part).wait_send()


def dense_body(tokens, expert_ids, gate_scales, w_gate, w_up, w_down):
    rows, width = tokens.shape
    sources = lax.axis_size("expert")
    line, steps, part_rows = sources // 2, 2 * sources, rows // 2
    experts = w_gate.shape[0] * sources
    half = w_gate.shape[2] // 2
    narrow, wide = jnp.bfloat16, jnp.float32
    top_k = expert_ids.shape[1]
    anywhere = pl.BlockSpec(memory_space=pl.ANY)
    return pl.pallas_call(
        dense_kernel,
        out_shape=jax.ShapeDtypeStruct((rows, width), narrow),
        in_specs=[anywhere] * 6,
        out_specs=anywhere,
        scratch_shapes=[
            pltpu.VMEM((top_k, rows), jnp.int32),
            pltpu.VMEM((top_k, rows), wide),
            pltpu.VMEM((rows, width), narrow),
            pltpu.VMEM((part_rows, width), wide),
            pltpu.VMEM((line, 2, 2, part_rows, width), narrow),
            pltpu.VMEM(w_gate.shape, narrow),
            pltpu.VMEM(w_up.shape, narrow),
            pltpu.VMEM(w_down.shape, narrow),
            pltpu.VMEM((line, 2, experts, rows), wide),
            pltpu.VMEM((steps, 2, 2, part_rows, half), narrow),
            pltpu.VMEM((steps, 2, 2, part_rows, half), narrow),
            pltpu.VMEM((2, 2, 2, part_rows, half), wide),
            pltpu.VMEM((steps, 2, part_rows, half), narrow),
            pltpu.VMEM((steps, 2, part_rows, half), narrow),
            pltpu.VMEM((3, 2, part_rows, half), wide),
            pltpu.VMEM((steps, 2, 2, part_rows, half), narrow),
            pltpu.VMEM((line, 2, part_rows, width), wide),
            pltpu.VMEM((line, 2, part_rows, width), narrow),
            pltpu.VMEM((line, 2, part_rows, width), narrow),
            pltpu.VMEM((line, 2, part_rows, width), narrow),
            pltpu.VMEM((line, 2, part_rows, width), narrow),
            pltpu.SemaphoreType.DMA((11,)),
            pltpu.SemaphoreType.REGULAR,
            pltpu.SemaphoreType.DMA((11, steps)),
            pltpu.SemaphoreType.DMA((11, steps)),
        ],
        compiler_params=pltpu.CompilerParams(
            collective_id=0, has_side_effects=True, vmem_limit_bytes=56 * 2**20
        ),
    )(tokens, expert_ids.T, gate_scales.T, w_gate, w_up, w_down)


def body(tokens, expert_ids, gate_scales, w_gate, w_up, w_down):
    rows, top_k = expert_ids.shape
    sources = lax.axis_size("expert")
    experts_all = w_gate.shape[0] * sources
    every_slot_used = 2 * rows * top_k // experts_all >= rows
    grouped = w_gate.shape[0] == 2 and lax.axis_size("dp") == 4 and sources == 8
    chosen = dense_body if every_slot_used and grouped else routed_body
    return chosen(tokens, expert_ids, gate_scales, w_gate, w_up, w_down)


def solution(mesh):
    in_specs = (
        P("expert", "dp"),
        P("expert", None),
        P("expert", None),
        P("expert", "dp", None),
        P("expert", "dp", None),
        P("expert", None, "dp"),
    )
    out_specs = P("expert", "dp")
    return jax.shard_map(body, mesh=mesh, in_specs=in_specs, out_specs=out_specs, check_vma=False)
```

```python
import functools

import jax
import jax.numpy as jnp
from jax import lax
from jax.experimental import pallas as pl
from jax.experimental.pallas import tpu as pltpu
from jax.sharding import PartitionSpec as P


def running_count(hits):
    count = hits.shape[-2]
    upto = jnp.tril(jnp.ones((count, count), jnp.bfloat16))
    sums = jnp.einsum("ij,...jm->...im", upto, hits.astype(jnp.bfloat16), preferred_element_type=jnp.float32)
    return sums.astype(jnp.int32)


def routed_body(tokens, expert_ids, gate_scales, w_gate, w_up, w_down):
    tok_rows, slice_width = tokens.shape
    top_k = expert_ids.shape[1]
    source_count = lax.axis_size("expert")
    local_experts = w_gate.shape[0]
    hidden_units = w_gate.shape[2]
    experts_all = local_experts * source_count
    capacity = 2 * tok_rows * top_k // experts_all
    assigns = tok_rows * top_k
    owner_rows = source_count * capacity
    flat_ids = expert_ids.reshape(assigns)
    catalog = jnp.arange(experts_all, dtype=jnp.int32)
    onehot = (flat_ids[:, None] == catalog[None, :]).astype(jnp.int32)
    rank_in = jnp.sum((running_count(onehot) - 1) * onehot, axis=1)
    owners = flat_ids // local_experts
    within = flat_ids % local_experts
    slot_index = within * owner_rows + owners * capacity + rank_in
    every_token = lax.all_gather(tokens, "expert", axis=0, tiled=True)
    every_id = lax.all_gather(expert_ids, "expert", axis=0, tiled=True)
    my_index = lax.axis_index("expert")
    grouped = every_id.reshape(source_count, assigns) - my_index * local_experts
    my_hits = (
        grouped[:, :, None] == jnp.arange(local_experts, dtype=jnp.int32)[None, None, :]
    ).astype(jnp.int32)
    my_ranks = jnp.sum((running_count(my_hits) - 1) * my_hits, axis=2)
    hit_count = jnp.sum(my_hits, axis=2)
    sources = jnp.arange(source_count, dtype=jnp.int32)[:, None]
    target = jnp.where(
        hit_count > 0,
        grouped * owner_rows + sources * capacity + my_ranks,
        local_experts * owner_rows,
    )
    anchor = sources * tok_rows + jnp.arange(assigns, dtype=jnp.int32)[None, :] // top_k
    token_total = source_count * tok_rows
    lookup = (
        jnp.full((local_experts * owner_rows,), token_total, jnp.int32)
        .at[target.reshape(-1)]
        .set(anchor.reshape(-1), mode="drop")
    )
    padded = jnp.concatenate([every_token, jnp.zeros((1, slice_width), tokens.dtype)], axis=0)
    arrived = padded[lookup].reshape(local_experts, owner_rows, slice_width)
    outputs = []
    for local_index in range(local_experts):
        rows_here = arrived[local_index]
        gate_here = w_gate[local_index]
        up_here = w_up[local_index]
        down_here = w_down[local_index]
        gate_part = jnp.dot(rows_here, gate_here, preferred_element_type=jnp.float32)
        up_part = jnp.dot(rows_here, up_here, preferred_element_type=jnp.float32)
        summed = lax.psum_scatter(
            jnp.concatenate([gate_part, up_part], axis=1).astype(jnp.bfloat16),
            "dp",
            scatter_dimension=0,
            tiled=True,
        ).astype(jnp.float32)
        hidden = (jax.nn.silu(summed[:, :hidden_units]) * summed[:, hidden_units:]).astype(
            jnp.bfloat16
        )
        outputs.append(
            jnp.dot(
                lax.all_gather(hidden, "dp", axis=0, tiled=True),
                down_here,
                preferred_element_type=jnp.float32,
            ).astype(jnp.bfloat16)
        )
    results = jnp.stack(outputs).reshape(local_experts, source_count, capacity, slice_width)
    returned = lax.all_to_all(results, "expert", split_axis=1, concat_axis=1, tiled=True)
    returned = returned.reshape(local_experts * owner_rows, slice_width)
    picked = returned[slot_index].reshape(tok_rows, top_k, slice_width)
    mixed = jnp.sum(gate_scales[:, :, None] * picked.astype(jnp.float32), axis=1)
    return mixed.astype(jnp.bfloat16)


MESH = pl.DeviceIdType.MESH
(
    CORE, ACROSS, HIDDEN_ACROSS, HIDDEN_CORE, HIDDEN_FORWARD, TOKEN_LINE, TOKEN_PAIR,
    SCALE_LINE, SCALE_PAIR, RESULT_PAIR, RESULT_LINE,
) = range(11)

ORDER = ((0, 0, 0), (0, 1, 0), (1, 0, 0), (1, 1, 0), (1, 1, 1), (2, 0, 0), (2, 1, 0), (2, 0, 1), (2, 1, 1), (3, 1, 0), (3, 0, 0), (3, 1, 1), (3, 0, 1), (1, 0, 1), (0, 1, 1), (0, 0, 1))
RELAY = {2: ((1, 0),), 3: ((1, 1),), 5: ((2, 0),), 7: ((2, 1),), 8: ((3, 0),), 10: ((3, 1),)}
SEND = {1: ((1, 1),), 3: ((2, 0),), 4: ((2, 1),), 6: ((3, 0),), 7: ((3, 1),)}
LATE_PAIR = 9
MERGE_AT = 12
MERGE = ((2, 0), (2, 1), (3, 0), (1, 0), (3, 1), (1, 1))


def pick(index, table):
    value = jnp.int32(table[0])
    for place in range(1, len(table)):
        value = jnp.where(index >= place, jnp.int32(table[place]), value)
    return value


def peer_of(me, step):
    total = 0
    for bit in (1, 2, 4):
        total = total + bit * ((me // bit + step // bit) % 2)
    return total


def chunk_at(step):
    code = pick(step, [away * 4 + pair * 2 + part for away, pair, part in ORDER])
    return code // 4, code // 2 % 2, code % 2


def dense_kernel(
    tokens, ids, scales, w_gate, w_up, w_down, out,
    ids_v, scales_v, out_v, first_half, tok_buf, gate_v, up_v, down_v, scale_buf,
    core_send, core_recv, kept_part, across_send, across_recv, kept_sum,
    hidden, kept_result, pair_send, pair_recv, line_send, line_recv, weight_sem, line_ready, send_sem, recv_sem,
):
    me = lax.axis_index("expert")
    slice_index = lax.axis_index("dp")
    core = slice_index % 2
    side = slice_index // 2
    other_core, other_side = 1 - core, 1 - side
    core_device = (me, side * 2 + other_core)
    side_device = (me, other_side * 2 + core)
    rows, width = tokens.shape
    part_rows = rows // 2
    half = hidden.shape[-1]
    line, steps = tok_buf.shape[0], core_send.shape[0]
    experts = scale_buf.shape[2]

    pair_device = (peer_of(me, 1), slice_index)

    def line_device(away):
        return (peer_of(me, 2 * away), slice_index)

    barrier = pltpu.get_barrier_semaphore()
    place = me // 2
    inner = (place == 1) | (place == 2)
    greeted = [core_device, side_device, pair_device, line_device(1)]
    for device in greeted:
        pl.semaphore_signal(barrier, inc=1, device_id=device, device_id_type=MESH)

    @pl.when(inner)
    def _():
        pl.semaphore_signal(barrier, inc=1, device_id=line_device(3), device_id_type=MESH)


    def load(place, source, target):
        return pltpu.make_async_copy(source, target, weight_sem.at[place])

    loads = [
        load(0, w_gate.at[other_core], gate_v.at[other_core]),
        load(1, w_up.at[other_core], up_v.at[other_core]),
        load(2, w_gate.at[core], gate_v.at[core]),
        load(3, w_up.at[core], up_v.at[core]),
        load(4, w_down, down_v),
    ]
    small = [
        load(5, tokens.at[0:part_rows], tok_buf.at[0, 0, 0]),
        load(6, tokens.at[part_rows:rows], tok_buf.at[0, 0, 1]),
        load(7, ids, ids_v),
        load(8, scales, scales_v),
    ]
    for each in small + loads[:2]:
        each.start()
    small[0].wait()
    @pl.when(inner)
    def _():
        pl.semaphore_wait(barrier, len(greeted) + 1)

    @pl.when(jnp.logical_not(inner))
    def _():
        pl.semaphore_wait(barrier, len(greeted))

    @pl.when(inner)
    def _():
        pl.semaphore_signal(line_ready, inc=1, device_id=line_device(3), device_id_type=MESH)


    def copy(kind, step, source, target, device):
        return pltpu.make_async_remote_copy(
            src_ref=source,
            dst_ref=target,
            send_sem=send_sem.at[kind, step],
            recv_sem=recv_sem.at[kind, step],
            device_id=device,
            device_id_type=MESH,
        )

    def line_token(away, part):
        return copy(
            TOKEN_LINE, away * 2 + part, tok_buf.at[0, 0, part], tok_buf.at[away, 0, part], line_device(away)
        )

    def pair_token(away, part):
        return copy(
            TOKEN_PAIR, away * 2 + part, tok_buf.at[away, 0, part], tok_buf.at[away, 1, part], pair_device
        )

    def line_scale(away):
        return copy(SCALE_LINE, away, scale_buf.at[0, 0], scale_buf.at[away, 0], line_device(away))

    def pair_scale(away):
        return copy(SCALE_PAIR, away, scale_buf.at[away, 0], scale_buf.at[away, 1], pair_device)

    def core_copy(step):
        return copy(CORE, step, core_send.at[step], core_recv.at[step], core_device)

    def across_copy(step):
        return copy(ACROSS, step, across_send.at[step], across_recv.at[step], side_device)

    def hidden_copy(kind, step, owner, part, device):
        piece = hidden.at[step, owner, part]
        return copy(kind, step, piece, piece, device)

    middle = width // 256 * 128
    columns = (pl.ds(0, middle), pl.ds(middle, width - middle))

    def pair_result(away, part, piece):
        where = (away, part, slice(None), columns[piece])
        return copy(
            RESULT_PAIR, (away * 2 + part) * 2 + piece, pair_send.at[where], pair_recv.at[where], pair_device
        )

    def line_result(away, part):
        return copy(
            RESULT_LINE, away * 2 + part, line_send.at[away, part], line_recv.at[away, part], line_device(away)
        )

    for each in loads[2:4]:
        each.start()
    pair_token(0, 0).start()
    line_token(1, 0).start()

    def project_other(step, block, ready=()):
        for which, weights in enumerate((gate_v, up_v)):
            for each in ready[which : which + 1]:
                each.wait()
            for cut in range(2):
                core_send[step, which, cut] = jnp.dot(
                    block, weights[other_core, :, cut * half : (cut + 1) * half],
                    preferred_element_type=jnp.float32,
                ).astype(jnp.bfloat16)
        core_copy(step).start()

    def project_own(step, block, ready=()):
        for which, weights in enumerate((gate_v, up_v)):
            for each in ready[which : which + 1]:
                each.wait()
            for cut in range(2):
                kept_part[step % 2, which, cut] = jnp.dot(
                    block, weights[core, :, cut * half : (cut + 1) * half],
                    preferred_element_type=jnp.float32,
                )

    def project(step):
        away, pair, part = chunk_at(step)

        @pl.when(pair == 1)
        def _():
            pair_token(away, part).wait_recv()

        block = tok_buf[away, pair, part]
        project_other(step, block)
        project_own(step, block)

    def add_core(step):
        core_copy(step).wait_recv()
        slot = step % 2
        for which in range(2):
            across_send[step, which] = (
                kept_part[slot, which, other_side]
                + core_recv[step, which, other_side].astype(jnp.float32)
            ).astype(jnp.bfloat16)
        across_copy(step).start()
        for which in range(2):
            kept_sum[step % 3, which] = kept_part[slot, which, side] + core_recv[
                step, which, side
            ].astype(jnp.float32)

    def activate(step):
        away, pair, part = chunk_at(step)

        @pl.when((part == 0) & (pair == 1))
        def _():
            pair_scale(away).wait_recv()

        across_copy(step).wait_recv()
        slot = step % 3
        shape = (part_rows, rows)
        chosen = lax.broadcasted_iota(jnp.int32, shape, 0) + part * part_rows == (
            lax.broadcasted_iota(jnp.int32, shape, 1)
        )
        row = scale_buf[away, pair, pl.ds(2 * me + core, 1), :]
        scale = jnp.sum(jnp.where(chosen, row, 0.0), axis=1, keepdims=True)
        gate = kept_sum[slot, 0] + across_recv[step, 0].astype(jnp.float32)
        up = kept_sum[slot, 1] + across_recv[step, 1].astype(jnp.float32)
        hidden[step, core, side] = (gate / (1.0 + jnp.exp(-gate)) * up * scale).astype(jnp.bfloat16)
        hidden_copy(HIDDEN_ACROSS, step, core, side, side_device).start()
        hidden_copy(HIDDEN_CORE, step, core, side, core_device).start()

    def forward(step):
        hidden_copy(HIDDEN_ACROSS, step, core, other_side, side_device).wait_recv()
        hidden_copy(HIDDEN_FORWARD, step, core, other_side, core_device).start()

    def share(step, cut, piece):
        low = pl.multiple_of(cut * half, half)
        return sum(
            jnp.dot(
                hidden[step, owner, cut], down_v[owner, pl.ds(low, half), columns[piece]],
                preferred_element_type=jnp.float32,
            )
            for owner in range(2)
        )

    def begin(step):
        @pl.when(step == 0)
        def _():
            loads[4].wait()

        hidden_copy(HIDDEN_CORE, step, other_core, side, core_device).wait_recv()
        for piece in range(2):
            first_half[:, columns[piece]] = share(step, side, piece)

    def finish(step):
        away, pair, part = chunk_at(step)
        hidden_copy(HIDDEN_FORWARD, step, other_core, other_side, core_device).wait_recv()
        for piece in range(2):
            value = first_half[:, columns[piece]] + share(step, other_side, piece)

            @pl.when(pair == 0)
            def _():
                kept_result[away, part, :, columns[piece]] = value

            @pl.when(pair == 1)
            def _():
                pair_send[away, part, :, columns[piece]] = value.astype(jnp.bfloat16)
                pair_result(away, part, piece).start()

    def merge(place):
        away, part = pick(place, [entry[0] for entry in MERGE]), pick(place, [entry[1] for entry in MERGE])
        for piece in range(2):
            pair_result(away, part, piece).wait_recv()
        line_send[away, part] = (
            kept_result[away, part] + pair_recv[away, part].astype(jnp.float32)
        ).astype(jnp.bfloat16)
        line_result(away, part).start()

    def store(part):
        rows_here = pl.ds(part * part_rows, part_rows)
        return pltpu.make_async_copy(out_v.at[rows_here], out.at[rows_here], weight_sem.at[9 + part])

    def conclude(part):
        for piece in range(2):
            pair_result(0, part, piece).wait_recv()
        value = kept_result[0, part] + pair_recv[0, part].astype(jnp.float32)
        for away in (2, 3, 1):
            line_result(away, part).wait_recv()
            value = value + line_recv[away, part].astype(jnp.float32)
        rows_here = pl.ds(part * part_rows, part_rows)
        out_v[rows_here] = value.astype(out_v.dtype)
        store(part).start()

    project_other(0, tok_buf[0, 0, 0], loads[0:2])
    project_own(0, tok_buf[0, 0, 0], loads[2:4])
    loads[4].start()
    for each in small[1:]:
        each.wait()
    which_expert = lax.broadcasted_iota(jnp.int32, (experts, rows), 0)
    table = jnp.zeros((experts, rows), jnp.float32)
    for k in range(ids_v.shape[0]):
        table = table + jnp.where(which_expert == ids_v[k : k + 1, :], scales_v[k : k + 1, :], 0.0)
    scale_buf[0, 0] = table
    pair_scale(0).start()
    line_scale(1).start()

    def staged(turn, lag, stage):
        @pl.when((turn >= lag) & (turn < steps + lag))
        def _():
            stage(turn - lag)

    def iteration(turn, carry):
        staged(turn, 1, add_core)
        for at, entries in RELAY.items():
            @pl.when(turn == at)
            def _():
                for away, part in entries:
                    line_token(away, part).wait_recv()
                    pair_token(away, part).start()
                    if part == 0:
                        line_scale(away).wait_recv()
                        pair_scale(away).start()
        @pl.when((turn == 2) & inner)
        def _():
            pl.semaphore_wait(line_ready, 1)
            pl.semaphore_signal(line_ready, inc=1, device_id=line_device(1), device_id_type=MESH)

        @pl.when((turn == 3) & jnp.logical_not(inner))
        def _():
            pl.semaphore_wait(line_ready, 1)

        for at, entries in SEND.items():
            @pl.when(turn == at)
            def _():
                for away, part in entries:
                    if away > 1 and part == 0:
                        line_scale(away).start()
                    line_token(away, part).start()

        @pl.when(turn == LATE_PAIR)
        def _():
            pair_token(0, 1).start()

        staged(turn, 0, project)
        @pl.when(turn == steps + 3)
        def _():
            conclude(0)

        staged(turn, 4, finish)
        @pl.when((turn >= MERGE_AT) & (turn < MERGE_AT + len(MERGE)))
        def _():
            merge(turn - MERGE_AT)

        staged(turn, 2, activate)
        staged(turn, 3, begin)
        staged(turn, 3, forward)

        return carry

    lax.fori_loop(1, steps + 4, iteration, 0)

    conclude(1)

    def drain(step, carry):
        core_copy(step).wait_send()
        across_copy(step).wait_send()
        hidden_copy(HIDDEN_ACROSS, step, core, side, side_device).wait_send()
        hidden_copy(HIDDEN_CORE, step, core, side, core_device).wait_send()
        hidden_copy(HIDDEN_FORWARD, step, core, other_side, core_device).wait_send()
        return carry

    lax.fori_loop(0, steps, drain, 0)
    for part in range(2):
        store(part).wait()
    for away in range(line):
        pair_scale(away).wait_send()
        if away > 0:
            line_scale(away).wait_send()
        for part in range(2):
            pair_token(away, part).wait_send()
            for piece in range(2):
                pair_result(away, part, piece).wait_send()
            if away > 0:
                line_token(away, part).wait_send()
                line_result(away, part).wait_send()


def dense_body(tokens, expert_ids, gate_scales, w_gate, w_up, w_down):
    rows, width = tokens.shape
    sources = lax.axis_size("expert")
    line, steps, part_rows = sources // 2, 2 * sources, rows // 2
    experts = w_gate.shape[0] * sources
    half = w_gate.shape[2] // 2
    narrow, wide = jnp.bfloat16, jnp.float32
    top_k = expert_ids.shape[1]
    anywhere = pl.BlockSpec(memory_space=pl.ANY)
    return pl.pallas_call(
        dense_kernel,
        out_shape=jax.ShapeDtypeStruct((rows, width), narrow),
        in_specs=[anywhere] * 6,
        out_specs=anywhere,
        scratch_shapes=[
            pltpu.VMEM((top_k, rows), jnp.int32),
            pltpu.VMEM((top_k, rows), wide),
            pltpu.VMEM((rows, width), narrow),
            pltpu.VMEM((part_rows, width), wide),
            pltpu.VMEM((line, 2, 2, part_rows, width), narrow),
            pltpu.VMEM(w_gate.shape, narrow),
            pltpu.VMEM(w_up.shape, narrow),
            pltpu.VMEM(w_down.shape, narrow),
            pltpu.VMEM((line, 2, experts, rows), wide),
            pltpu.VMEM((steps, 2, 2, part_rows, half), narrow),
            pltpu.VMEM((steps, 2, 2, part_rows, half), narrow),
            pltpu.VMEM((2, 2, 2, part_rows, half), wide),
            pltpu.VMEM((steps, 2, part_rows, half), narrow),
            pltpu.VMEM((steps, 2, part_rows, half), narrow),
            pltpu.VMEM((3, 2, part_rows, half), wide),
            pltpu.VMEM((steps, 2, 2, part_rows, half), narrow),
            pltpu.VMEM((line, 2, part_rows, width), wide),
            pltpu.VMEM((line, 2, part_rows, width), narrow),
            pltpu.VMEM((line, 2, part_rows, width), narrow),
            pltpu.VMEM((line, 2, part_rows, width), narrow),
            pltpu.VMEM((line, 2, part_rows, width), narrow),
            pltpu.SemaphoreType.DMA((11,)),
            pltpu.SemaphoreType.REGULAR,
            pltpu.SemaphoreType.DMA((11, steps)),
            pltpu.SemaphoreType.DMA((11, steps)),
        ],
        compiler_params=pltpu.CompilerParams(
            collective_id=0, has_side_effects=True, vmem_limit_bytes=56 * 2**20
        ),
    )(tokens, expert_ids.T, gate_scales.T, w_gate, w_up, w_down)


def body(tokens, expert_ids, gate_scales, w_gate, w_up, w_down):
    rows, top_k = expert_ids.shape
    sources = lax.axis_size("expert")
    experts_all = w_gate.shape[0] * sources
    every_slot_used = 2 * rows * top_k // experts_all >= rows
    grouped = w_gate.shape[0] == 2 and lax.axis_size("dp") == 4 and sources == 8
    chosen = dense_body if every_slot_used and grouped else routed_body
    return chosen(tokens, expert_ids, gate_scales, w_gate, w_up, w_down)


def solution(mesh):
    in_specs = (
        P("expert", "dp"),
        P("expert", None),
        P("expert", None),
        P("expert", "dp", None),
        P("expert", "dp", None),
        P("expert", None, "dp"),
    )
    out_specs = P("expert", "dp")
    return jax.shard_map(body, mesh=mesh, in_specs=in_specs, out_specs=out_specs, check_vma=False)
```

```python
import functools

import jax
import jax.numpy as jnp
from jax import lax
from jax.experimental import pallas as pl
from jax.experimental.pallas import tpu as pltpu
from jax.sharding import PartitionSpec as P


def running_count(hits):
    count = hits.shape[-2]
    upto = jnp.tril(jnp.ones((count, count), jnp.bfloat16))
    sums = jnp.einsum("ij,...jm->...im", upto, hits.astype(jnp.bfloat16), preferred_element_type=jnp.float32)
    return sums.astype(jnp.int32)


def routed_body(tokens, expert_ids, gate_scales, w_gate, w_up, w_down):
    tok_rows, slice_width = tokens.shape
    top_k = expert_ids.shape[1]
    source_count = lax.axis_size("expert")
    local_experts = w_gate.shape[0]
    hidden_units = w_gate.shape[2]
    experts_all = local_experts * source_count
    capacity = 2 * tok_rows * top_k // experts_all
    assigns = tok_rows * top_k
    owner_rows = source_count * capacity
    flat_ids = expert_ids.reshape(assigns)
    catalog = jnp.arange(experts_all, dtype=jnp.int32)
    onehot = (flat_ids[:, None] == catalog[None, :]).astype(jnp.int32)
    rank_in = jnp.sum((running_count(onehot) - 1) * onehot, axis=1)
    owners = flat_ids // local_experts
    within = flat_ids % local_experts
    slot_index = within * owner_rows + owners * capacity + rank_in
    every_token = lax.all_gather(tokens, "expert", axis=0, tiled=True)
    every_id = lax.all_gather(expert_ids, "expert", axis=0, tiled=True)
    my_index = lax.axis_index("expert")
    grouped = every_id.reshape(source_count, assigns) - my_index * local_experts
    my_hits = (
        grouped[:, :, None] == jnp.arange(local_experts, dtype=jnp.int32)[None, None, :]
    ).astype(jnp.int32)
    my_ranks = jnp.sum((running_count(my_hits) - 1) * my_hits, axis=2)
    hit_count = jnp.sum(my_hits, axis=2)
    sources = jnp.arange(source_count, dtype=jnp.int32)[:, None]
    target = jnp.where(
        hit_count > 0,
        grouped * owner_rows + sources * capacity + my_ranks,
        local_experts * owner_rows,
    )
    anchor = sources * tok_rows + jnp.arange(assigns, dtype=jnp.int32)[None, :] // top_k
    token_total = source_count * tok_rows
    lookup = (
        jnp.full((local_experts * owner_rows,), token_total, jnp.int32)
        .at[target.reshape(-1)]
        .set(anchor.reshape(-1), mode="drop")
    )
    padded = jnp.concatenate([every_token, jnp.zeros((1, slice_width), tokens.dtype)], axis=0)
    arrived = padded[lookup].reshape(local_experts, owner_rows, slice_width)
    outputs = []
    for local_index in range(local_experts):
        rows_here = arrived[local_index]
        gate_here = w_gate[local_index]
        up_here = w_up[local_index]
        down_here = w_down[local_index]
        gate_part = jnp.dot(rows_here, gate_here, preferred_element_type=jnp.float32)
        up_part = jnp.dot(rows_here, up_here, preferred_element_type=jnp.float32)
        summed = lax.psum_scatter(
            jnp.concatenate([gate_part, up_part], axis=1).astype(jnp.bfloat16),
            "dp",
            scatter_dimension=0,
            tiled=True,
        ).astype(jnp.float32)
        hidden = (jax.nn.silu(summed[:, :hidden_units]) * summed[:, hidden_units:]).astype(
            jnp.bfloat16
        )
        outputs.append(
            jnp.dot(
                lax.all_gather(hidden, "dp", axis=0, tiled=True),
                down_here,
                preferred_element_type=jnp.float32,
            ).astype(jnp.bfloat16)
        )
    results = jnp.stack(outputs).reshape(local_experts, source_count, capacity, slice_width)
    returned = lax.all_to_all(results, "expert", split_axis=1, concat_axis=1, tiled=True)
    returned = returned.reshape(local_experts * owner_rows, slice_width)
    picked = returned[slot_index].reshape(tok_rows, top_k, slice_width)
    mixed = jnp.sum(gate_scales[:, :, None] * picked.astype(jnp.float32), axis=1)
    return mixed.astype(jnp.bfloat16)


MESH = pl.DeviceIdType.MESH
(
    CORE, ACROSS, HIDDEN_ACROSS, HIDDEN_CORE, HIDDEN_FORWARD, TOKEN_LINE, TOKEN_PAIR,
    SCALE_LINE, SCALE_PAIR, RESULT_PAIR, RESULT_LINE,
) = range(11)

ORDER = ((0, 0, 0), (0, 1, 0), (1, 0, 0), (1, 1, 0), (1, 1, 1), (2, 0, 0), (2, 1, 0), (2, 0, 1), (2, 1, 1), (3, 1, 0), (3, 0, 0), (3, 1, 1), (3, 0, 1), (1, 0, 1), (0, 1, 1), (0, 0, 1))
RELAY = {2: ((1, 0),), 3: ((1, 1),), 5: ((2, 0),), 6: ((2, 1),), 8: ((3, 0),), 9: ((3, 1),)}
SEND = {1: ((1, 1),), 3: ((2, 0),), 4: ((2, 1),), 6: ((3, 0),), 7: ((3, 1),)}
LATE_PAIR = 9
MERGE_AT = 12
MERGE = ((2, 0), (2, 1), (3, 0), (1, 0), (3, 1), (1, 1))


def pick(index, table):
    value = jnp.int32(table[0])
    for place in range(1, len(table)):
        value = jnp.where(index >= place, jnp.int32(table[place]), value)
    return value


def peer_of(me, step):
    total = 0
    for bit in (1, 2, 4):
        total = total + bit * ((me // bit + step // bit) % 2)
    return total


def chunk_at(step):
    code = pick(step, [away * 4 + pair * 2 + part for away, pair, part in ORDER])
    return code // 4, code // 2 % 2, code % 2


def dense_kernel(
    tokens, ids, scales, w_gate, w_up, w_down, out,
    ids_v, scales_v, out_v, first_half, tok_buf, gate_v, up_v, down_v, scale_buf,
    core_send, core_recv, kept_part, across_send, across_recv, kept_sum,
    hidden, kept_result, pair_send, pair_recv, line_send, line_recv, weight_sem, line_ready, send_sem, recv_sem,
):
    me = lax.axis_index("expert")
    slice_index = lax.axis_index("dp")
    core = slice_index % 2
    side = slice_index // 2
    other_core, other_side = 1 - core, 1 - side
    core_device = (me, side * 2 + other_core)
    side_device = (me, other_side * 2 + core)
    rows, width = tokens.shape
    part_rows = rows // 2
    half = hidden.shape[-1]
    line, steps = tok_buf.shape[0], core_send.shape[0]
    experts = scale_buf.shape[2]

    pair_device = (peer_of(me, 1), slice_index)

    def line_device(away):
        return (peer_of(me, 2 * away), slice_index)

    barrier = pltpu.get_barrier_semaphore()
    place = me // 2
    inner = (place == 1) | (place == 2)
    greeted = [core_device, side_device, pair_device, line_device(1)]
    for device in greeted:
        pl.semaphore_signal(barrier, inc=1, device_id=device, device_id_type=MESH)

    @pl.when(inner)
    def _():
        pl.semaphore_signal(barrier, inc=1, device_id=line_device(3), device_id_type=MESH)


    def load(place, source, target):
        return pltpu.make_async_copy(source, target, weight_sem.at[place])

    loads = [
        load(0, w_gate.at[other_core], gate_v.at[other_core]),
        load(1, w_up.at[other_core], up_v.at[other_core]),
        load(2, w_gate.at[core], gate_v.at[core]),
        load(3, w_up.at[core], up_v.at[core]),
        load(4, w_down, down_v),
    ]
    small = [
        load(5, tokens.at[0:part_rows], tok_buf.at[0, 0, 0]),
        load(6, tokens.at[part_rows:rows], tok_buf.at[0, 0, 1]),
        load(7, ids, ids_v),
        load(8, scales, scales_v),
    ]
    for each in small + loads[:2]:
        each.start()
    small[0].wait()
    @pl.when(inner)
    def _():
        pl.semaphore_wait(barrier, len(greeted) + 1)

    @pl.when(jnp.logical_not(inner))
    def _():
        pl.semaphore_wait(barrier, len(greeted))

    @pl.when(inner)
    def _():
        pl.semaphore_signal(line_ready, inc=1, device_id=line_device(3), device_id_type=MESH)


    def copy(kind, step, source, target, device):
        return pltpu.make_async_remote_copy(
            src_ref=source,
            dst_ref=target,
            send_sem=send_sem.at[kind, step],
            recv_sem=recv_sem.at[kind, step],
            device_id=device,
            device_id_type=MESH,
        )

    def line_token(away, part):
        return copy(
            TOKEN_LINE, away * 2 + part, tok_buf.at[0, 0, part], tok_buf.at[away, 0, part], line_device(away)
        )

    def pair_token(away, part):
        return copy(
            TOKEN_PAIR, away * 2 + part, tok_buf.at[away, 0, part], tok_buf.at[away, 1, part], pair_device
        )

    def line_scale(away):
        return copy(SCALE_LINE, away, scale_buf.at[0, 0], scale_buf.at[away, 0], line_device(away))

    def pair_scale(away):
        return copy(SCALE_PAIR, away, scale_buf.at[away, 0], scale_buf.at[away, 1], pair_device)

    def core_copy(step):
        return copy(CORE, step, core_send.at[step], core_recv.at[step], core_device)

    def across_copy(step):
        return copy(ACROSS, step, across_send.at[step], across_recv.at[step], side_device)

    def hidden_copy(kind, step, owner, part, device):
        piece = hidden.at[step, owner, part]
        return copy(kind, step, piece, piece, device)

    middle = width // 256 * 128
    columns = (pl.ds(0, middle), pl.ds(middle, width - middle))

    def pair_result(away, part, piece):
        where = (away, part, slice(None), columns[piece])
        return copy(
            RESULT_PAIR, (away * 2 + part) * 2 + piece, pair_send.at[where], pair_recv.at[where], pair_device
        )

    def line_result(away, part):
        return copy(
            RESULT_LINE, away * 2 + part, line_send.at[away, part], line_recv.at[away, part], line_device(away)
        )

    for each in loads[2:4]:
        each.start()
    pair_token(0, 0).start()
    line_token(1, 0).start()

    def project_other(step, block, ready=()):
        for which, weights in enumerate((gate_v, up_v)):
            for each in ready[which : which + 1]:
                each.wait()
            for cut in range(2):
                core_send[step, which, cut] = jnp.dot(
                    block, weights[other_core, :, cut * half : (cut + 1) * half],
                    preferred_element_type=jnp.float32,
                ).astype(jnp.bfloat16)
        core_copy(step).start()

    def project_own(step, block, ready=()):
        for which, weights in enumerate((gate_v, up_v)):
            for each in ready[which : which + 1]:
                each.wait()
            for cut in range(2):
                kept_part[step % 2, which, cut] = jnp.dot(
                    block, weights[core, :, cut * half : (cut + 1) * half],
                    preferred_element_type=jnp.float32,
                )

    def project(step):
        away, pair, part = chunk_at(step)

        @pl.when(pair == 1)
        def _():
            pair_token(away, part).wait_recv()

        block = tok_buf[away, pair, part]
        project_other(step, block)
        project_own(step, block)

    def add_core(step):
        core_copy(step).wait_recv()
        slot = step % 2
        for which in range(2):
            across_send[step, which] = (
                kept_part[slot, which, other_side]
                + core_recv[step, which, other_side].astype(jnp.float32)
            ).astype(jnp.bfloat16)
        across_copy(step).start()
        for which in range(2):
            kept_sum[step % 3, which] = kept_part[slot, which, side] + core_recv[
                step, which, side
            ].astype(jnp.float32)

    def activate(step):
        away, pair, part = chunk_at(step)

        @pl.when((part == 0) & (pair == 1))
        def _():
            pair_scale(away).wait_recv()

        across_copy(step).wait_recv()
        slot = step % 3
        shape = (part_rows, rows)
        chosen = lax.broadcasted_iota(jnp.int32, shape, 0) + part * part_rows == (
            lax.broadcasted_iota(jnp.int32, shape, 1)
        )
        row = scale_buf[away, pair, pl.ds(2 * me + core, 1), :]
        scale = jnp.sum(jnp.where(chosen, row, 0.0), axis=1, keepdims=True)
        gate = kept_sum[slot, 0] + across_recv[step, 0].astype(jnp.float32)
        up = kept_sum[slot, 1] + across_recv[step, 1].astype(jnp.float32)
        hidden[step, core, side] = (gate / (1.0 + jnp.exp(-gate)) * up * scale).astype(jnp.bfloat16)
        hidden_copy(HIDDEN_ACROSS, step, core, side, side_device).start()
        hidden_copy(HIDDEN_CORE, step, core, side, core_device).start()

    def forward(step):
        hidden_copy(HIDDEN_ACROSS, step, core, other_side, side_device).wait_recv()
        hidden_copy(HIDDEN_FORWARD, step, core, other_side, core_device).start()

    def share(step, cut, piece):
        low = pl.multiple_of(cut * half, half)
        return sum(
            jnp.dot(
                hidden[step, owner, cut], down_v[owner, pl.ds(low, half), columns[piece]],
                preferred_element_type=jnp.float32,
            )
            for owner in range(2)
        )

    def begin(step):
        @pl.when(step == 0)
        def _():
            loads[4].wait()

        hidden_copy(HIDDEN_CORE, step, other_core, side, core_device).wait_recv()
        for piece in range(2):
            first_half[:, columns[piece]] = share(step, side, piece)

    def finish(step):
        away, pair, part = chunk_at(step)
        hidden_copy(HIDDEN_FORWARD, step, other_core, other_side, core_device).wait_recv()
        for piece in range(2):
            value = first_half[:, columns[piece]] + share(step, other_side, piece)

            @pl.when(pair == 0)
            def _():
                kept_result[away, part, :, columns[piece]] = value

            @pl.when(pair == 1)
            def _():
                pair_send[away, part, :, columns[piece]] = value.astype(jnp.bfloat16)
                pair_result(away, part, piece).start()

    def merge(place):
        away, part = pick(place, [entry[0] for entry in MERGE]), pick(place, [entry[1] for entry in MERGE])
        for piece in range(2):
            pair_result(away, part, piece).wait_recv()
        line_send[away, part] = (
            kept_result[away, part] + pair_recv[away, part].astype(jnp.float32)
        ).astype(jnp.bfloat16)
        line_result(away, part).start()

    def store(part):
        rows_here = pl.ds(part * part_rows, part_rows)
        return pltpu.make_async_copy(out_v.at[rows_here], out.at[rows_here], weight_sem.at[9 + part])

    def conclude(part):
        for piece in range(2):
            pair_result(0, part, piece).wait_recv()
        value = kept_result[0, part] + pair_recv[0, part].astype(jnp.float32)
        for away in (2, 3, 1):
            line_result(away, part).wait_recv()
            value = value + line_recv[away, part].astype(jnp.float32)
        rows_here = pl.ds(part * part_rows, part_rows)
        out_v[rows_here] = value.astype(out_v.dtype)
        store(part).start()

    project_other(0, tok_buf[0, 0, 0], loads[0:2])
    project_own(0, tok_buf[0, 0, 0], loads[2:4])
    loads[4].start()
    for each in small[1:]:
        each.wait()
    which_expert = lax.broadcasted_iota(jnp.int32, (experts, rows), 0)
    table = jnp.zeros((experts, rows), jnp.float32)
    for k in range(ids_v.shape[0]):
        table = table + jnp.where(which_expert == ids_v[k : k + 1, :], scales_v[k : k + 1, :], 0.0)
    scale_buf[0, 0] = table
    pair_scale(0).start()
    line_scale(1).start()

    def staged(turn, lag, stage):
        @pl.when((turn >= lag) & (turn < steps + lag))
        def _():
            stage(turn - lag)

    def iteration(turn, carry):
        staged(turn, 1, add_core)
        for at, entries in RELAY.items():
            @pl.when(turn == at)
            def _():
                for away, part in entries:
                    line_token(away, part).wait_recv()
                    pair_token(away, part).start()
                    if part == 0:
                        line_scale(away).wait_recv()
                        pair_scale(away).start()
        @pl.when((turn == 2) & inner)
        def _():
            pl.semaphore_wait(line_ready, 1)
            pl.semaphore_signal(line_ready, inc=1, device_id=line_device(1), device_id_type=MESH)

        @pl.when((turn == 3) & jnp.logical_not(inner))
        def _():
            pl.semaphore_wait(line_ready, 1)

        for at, entries in SEND.items():
            @pl.when(turn == at)
            def _():
                for away, part in entries:
                    if away > 1 and part == 0:
                        line_scale(away).start()
                    line_token(away, part).start()

        @pl.when(turn == LATE_PAIR)
        def _():
            pair_token(0, 1).start()

        staged(turn, 0, project)
        @pl.when(turn == steps + 3)
        def _():
            conclude(0)

        staged(turn, 4, finish)
        @pl.when((turn >= MERGE_AT) & (turn < MERGE_AT + len(MERGE)))
        def _():
            merge(turn - MERGE_AT)

        staged(turn, 2, activate)
        staged(turn, 3, begin)
        staged(turn, 3, forward)

        return carry

    lax.fori_loop(1, steps + 4, iteration, 0)

    conclude(1)

    def drain(step, carry):
        core_copy(step).wait_send()
        across_copy(step).wait_send()
        hidden_copy(HIDDEN_ACROSS, step, core, side, side_device).wait_send()
        hidden_copy(HIDDEN_CORE, step, core, side, core_device).wait_send()
        hidden_copy(HIDDEN_FORWARD, step, core, other_side, core_device).wait_send()
        return carry

    lax.fori_loop(0, steps, drain, 0)
    for part in range(2):
        store(part).wait()
    for away in range(line):
        pair_scale(away).wait_send()
        if away > 0:
            line_scale(away).wait_send()
        for part in range(2):
            pair_token(away, part).wait_send()
            for piece in range(2):
                pair_result(away, part, piece).wait_send()
            if away > 0:
                line_token(away, part).wait_send()
                line_result(away, part).wait_send()


def dense_body(tokens, expert_ids, gate_scales, w_gate, w_up, w_down):
    rows, width = tokens.shape
    sources = lax.axis_size("expert")
    line, steps, part_rows = sources // 2, 2 * sources, rows // 2
    experts = w_gate.shape[0] * sources
    half = w_gate.shape[2] // 2
    narrow, wide = jnp.bfloat16, jnp.float32
    top_k = expert_ids.shape[1]
    anywhere = pl.BlockSpec(memory_space=pl.ANY)
    return pl.pallas_call(
        dense_kernel,
        out_shape=jax.ShapeDtypeStruct((rows, width), narrow),
        in_specs=[anywhere] * 6,
        out_specs=anywhere,
        scratch_shapes=[
            pltpu.VMEM((top_k, rows), jnp.int32),
            pltpu.VMEM((top_k, rows), wide),
            pltpu.VMEM((rows, width), narrow),
            pltpu.VMEM((part_rows, width), wide),
            pltpu.VMEM((line, 2, 2, part_rows, width), narrow),
            pltpu.VMEM(w_gate.shape, narrow),
            pltpu.VMEM(w_up.shape, narrow),
            pltpu.VMEM(w_down.shape, narrow),
            pltpu.VMEM((line, 2, experts, rows), wide),
            pltpu.VMEM((steps, 2, 2, part_rows, half), narrow),
            pltpu.VMEM((steps, 2, 2, part_rows, half), narrow),
            pltpu.VMEM((2, 2, 2, part_rows, half), wide),
            pltpu.VMEM((steps, 2, part_rows, half), narrow),
            pltpu.VMEM((steps, 2, part_rows, half), narrow),
            pltpu.VMEM((3, 2, part_rows, half), wide),
            pltpu.VMEM((steps, 2, 2, part_rows, half), narrow),
            pltpu.VMEM((line, 2, part_rows, width), wide),
            pltpu.VMEM((line, 2, part_rows, width), narrow),
            pltpu.VMEM((line, 2, part_rows, width), narrow),
            pltpu.VMEM((line, 2, part_rows, width), narrow),
            pltpu.VMEM((line, 2, part_rows, width), narrow),
            pltpu.SemaphoreType.DMA((11,)),
            pltpu.SemaphoreType.REGULAR,
            pltpu.SemaphoreType.DMA((11, steps)),
            pltpu.SemaphoreType.DMA((11, steps)),
        ],
        compiler_params=pltpu.CompilerParams(
            collective_id=0, has_side_effects=True, vmem_limit_bytes=56 * 2**20
        ),
    )(tokens, expert_ids.T, gate_scales.T, w_gate, w_up, w_down)


def body(tokens, expert_ids, gate_scales, w_gate, w_up, w_down):
    rows, top_k = expert_ids.shape
    sources = lax.axis_size("expert")
    experts_all = w_gate.shape[0] * sources
    every_slot_used = 2 * rows * top_k // experts_all >= rows
    grouped = w_gate.shape[0] == 2 and lax.axis_size("dp") == 4 and sources == 8
    chosen = dense_body if every_slot_used and grouped else routed_body
    return chosen(tokens, expert_ids, gate_scales, w_gate, w_up, w_down)


def solution(mesh):
    in_specs = (
        P("expert", "dp"),
        P("expert", None),
        P("expert", None),
        P("expert", "dp", None),
        P("expert", "dp", None),
        P("expert", None, "dp"),
    )
    out_specs = P("expert", "dp")
    return jax.shard_map(body, mesh=mesh, in_specs=in_specs, out_specs=out_specs, check_vma=False)
```
